32 devices in a mesh: member: 4 (over x, core), tile: 8 (over z, y).
Axes of the slice: x: 2, y: 2, z: 4, core: 2. Of those that a mesh axis runs over, the one named last changes fastest.
Arguments:
- fields: float32 [8, 48, 3072], P('member', 'tile'), may hold values from 0 to 15, as said below
Outputs:
- frequencies: float32 [26, 48, 3072], P(None, 'tile', 'member')
The draws below stay inside these ranges and needn't reach their ends.
Inputs may be any that keep to these rules, and one draw needn't show every extreme that they name: `fields`: every entry is a whole number.
All inputs are finite; a program needn't handle non-finite values.
Results may differ from the reference program's by a relative error of at most 0.0003.
Values may be sent and summed in bfloat16 or wider, within the bound.
No kernel may reach another device: no remote copies, remote signals or barrier semaphores. Data moves between devices by JAX's collectives and lax.ppermute only.
A program may use at most 64 MiB of HBM per device.

```python
import jax
import jax.numpy as jnp
from jax import lax

NZ = 192
MEMBERS = 8
NX = 48
NY = 16
NDIR = 26


def draw_fields(key, part):
    return jax.random.randint(key, (MEMBERS, NX, NY * NZ), 0, 16).astype(jnp.float32)


def setup_inputs(seed: int = 0) -> dict:
    splits = jax.random.split(jax.random.key(seed), 2)
    fields = draw_fields(jax.random.fold_in(splits[1], 71), 0)
    return {"fields": fields}


barrier_level = 1000000.0
offset_table = [(a, b, c) for a in (-1, 0, 1) for b in (-1, 0, 1) for c in (-1, 0, 1) if (a, b, c) != (0, 0, 0)]


def direction_counts(padded):
    planes = padded.shape[1] - 2
    rows_here = padded.shape[2] - 2
    depth = padded.shape[3] - 2
    center = padded[:, 1:planes + 1, 1:rows_here + 1, 1:depth + 1]
    descents = []
    for offset in offset_table:
        moved = padded[:, 1 + offset[0]:1 + offset[0] + planes, 1 + offset[1]:1 + offset[1] + rows_here, 1 + offset[2]:1 + offset[2] + depth]
        descents.append(moved - center)
    deepest = jnp.zeros_like(center)
    for drop in descents:
        deepest = jnp.minimum(deepest, drop)
    claimed = jnp.zeros(center.shape, bool)
    tallies = []
    for drop in descents:
        chosen = (drop == deepest) & (deepest < 0) & jnp.logical_not(claimed)
        tallies.append(jnp.sum(chosen.astype(jnp.float32), axis=0))
        claimed = claimed | chosen
    return jnp.stack(tallies)


def reference(fields):
    shaped = fields.reshape(MEMBERS, NX, NY, NZ)
    padded_all = jnp.pad(shaped, ((0, 0), (1, 1), (1, 1), (1, 1)), constant_values=barrier_level)

    def accumulate(total, padded):
        return total + direction_counts(padded[None]), None

    start = jnp.zeros((NDIR, NX, NY, NZ), jnp.float32)
    total, unused = lax.scan(accumulate, start, padded_all)
    return (total / MEMBERS).reshape(NDIR, NX, NY * NZ)
```

```python
import functools

import jax
import jax.numpy as jnp
from jax import lax
from jax.experimental import pallas as pl
from jax.experimental.pallas import tpu as pltpu
from jax.sharding import PartitionSpec as P

NZ = 192
LANES = 128
EDGE = 3
PAD = 64.0
FAR = 4096.0
VMEM = pl.BlockSpec(memory_space=pltpu.VMEM)
PARAMS = pltpu.CompilerParams(vmem_limit_bytes=8 << 20)


def permute(value, pairs):
    return lax.ppermute(value, ("member", "tile"), pairs)


def pairs_of(members, tiles, partner):
    pairs = []
    for m in range(members):
        for t in range(tiles):
            to_m, to_t = partner(m, t)
            pairs.append((m * tiles + t, to_m * tiles + to_t))
    return pairs


def even_partner(members, tiles):
    return pairs_of(members, tiles, lambda m, t: (m, t ^ 1))


def odd_partner(members, tiles):
    def partner(m, t):
        if t == 0 or t == tiles - 1:
            return m ^ (members // 2), t
        return m, (t + 1 if t % 2 else t - 1)

    return pairs_of(members, tiles, partner)


def cut_kernel(mloc, width, step, members, src, *rest):
    outs, padded = rest[:members], rest[members]
    planes, rows = src.shape[0], src.shape[1]
    lead = 8
    assert lead >= EDGE * mloc
    me = lax.axis_index("member")
    for p in range(planes):
        padded[p, 0:lead, :] = jnp.full((lead, LANES), PAD, jnp.float32)
        padded[p, lead : lead + rows, :] = src[p]
        padded[p, lead + rows : lead + rows + lead, :] = jnp.full((lead, LANES), PAD, jnp.float32)
    for k in range(members):
        base = (me ^ k) * (step * mloc) + lead - EDGE * mloc
        for p in range(planes):
            for i in range(mloc):
                cut = padded[p, pl.ds(base + i, width, stride=mloc), :]
                outs[k][p, i * width : (i + 1) * width, :] = cut.astype(jnp.bfloat16)


def edge_kernel(members, *refs):
    bufs, (send_even, send_odd) = refs[:members], refs[members:]
    planes, rows = bufs[0].shape[0], bufs[0].shape[1]
    odd = lax.axis_index("tile") % 2
    for k in range(members):
        send_even[k * rows : (k + 1) * rows, :] = bufs[k][(planes - 1) * (1 - odd)]
        send_odd[k * rows : (k + 1) * rows, :] = bufs[k][(planes - 1) * odd]


def count_kernel(members, mloc, width, step, *refs):
    bufs = refs[:members]
    got_even, got_odd, out, stage = refs[members:]
    planes, rows = bufs[0].shape[0], bufs[0].shape[1]
    total = members * mloc
    tile, tiles = lax.axis_index("tile"), lax.axis_size("tile")
    odd = tile % 2
    for k in range(members):
        for p in range(planes):
            stage[p + 1, k * rows : (k + 1) * rows, :] = bufs[k][p].astype(jnp.float32)
    stage[(planes + 1) * (1 - odd)] = got_even[...].astype(jnp.float32)
    stage[(planes + 1) * odd] = got_odd[...].astype(jnp.float32)

    @pl.when(tile == 0)
    def _():
        stage[0] = jnp.full(stage.shape[1:], PAD, jnp.float32)

    @pl.when(tile == tiles - 1)
    def _():
        stage[planes + 1] = jnp.full(stage.shape[1:], PAD, jnp.float32)

    lane = lax.broadcasted_iota(jnp.int32, (8, LANES), 1)
    sub = lax.broadcasted_iota(jnp.int32, (8, LANES), 0)
    low, first, last = lane < 64, lane == 0, lane == LANES - 1
    at64, at63 = lane == 64, lane == 63
    groups = -(-out.shape[1] // 8)

    def plane_keys(p, group):
        value = {
            j: stage[p, pl.ds(group * 8 * width + j, 8, stride=width), :] * 32.0
            for j in range(EDGE - 2, EDGE + step + 2)
        }
        keys = {}
        for j, here in value.items():
            before = pltpu.roll(here, 1, 1)
            after = pltpu.roll(here, LANES - 1, 1)
            phase = j % 3
            if phase == 0:
                before = jnp.where(first, FAR, before)
            elif j - 1 in value:
                before = jnp.where(first, pltpu.roll(value[j - 1], 1, 1), before)
            if phase == 2:
                after = jnp.where(last, FAR, after)
            elif j + 1 in value:
                after = jnp.where(last, pltpu.roll(value[j + 1], LANES - 1, 1), after)
            if phase == 1:
                before = jnp.where(at64, FAR, before)
                after = jnp.where(at63, FAR, after)
            keys[j] = jnp.minimum(jnp.minimum(before, here + 1.0), after + 2.0)
        turned = {j: pltpu.roll(key, 64, 1) for j, key in keys.items()}
        row_before = {
            j: jnp.where(low, turned[j - 2], turned[j - 1]) for j in range(EDGE, EDGE + step + 3)
        }
        result = []
        for j in range(EDGE, EDGE + step):
            key = jnp.minimum(row_before[j], keys[j] + 3.0)
            result.append((jnp.minimum(key, row_before[j + 3] + 6.0), value[j]))
        return result

    for group in range(total // 8):
        layers = [plane_keys(p, group) for p in range(planes + 2)]
        for p in range(planes):
            for j in range(step):
                best = jnp.minimum(layers[p][j][0], layers[p + 1][j][0] + 9.0)
                best = jnp.minimum(best, layers[p + 2][j][0] + 18.0)
                found = best < layers[p + 1][j][1]
                code = best.astype(jnp.int32) & 31
                code = jnp.where(code > 13, code - 1, code)
                bit = jnp.where(found, jnp.int32(1) << ((code & 7) * 4), 0)
                kind = code >> 3
                for g in range(groups):
                    word = jnp.where(kind == g, bit, 0)
                    word = word + pltpu.roll(word, 4, 0)
                    word = word + pltpu.roll(word, 2, 0)
                    word = word + pltpu.roll(word, 1, 0)
                    share = ((word >> (sub * 4)) & 15).astype(jnp.float32) * (1.0 / total)
                    n = min(8, out.shape[1] - 8 * g)
                    at = (p, slice(8 * g, 8 * g + n), slice(j * LANES, (j + 1) * LANES))
                    if group == 0:
                        out[at] = share[:n]
                    else:
                        out[at] = out[at] + share[:n]


def local(members, tiles, fields):
    mloc, planes, cols = fields.shape
    step = cols // members // LANES
    width = step + 2 * EDGE
    spread = cols // LANES
    view = fields.reshape(mloc, planes, spread, LANES).transpose(1, 2, 0, 3)
    view = view.reshape(planes, spread * mloc, LANES)
    rows = mloc * width
    cuts = pl.pallas_call(
        functools.partial(cut_kernel, mloc, width, step, members),
        out_shape=[jax.ShapeDtypeStruct((planes, rows, LANES), jnp.bfloat16)] * members,
        in_specs=[VMEM],
        out_specs=[VMEM] * members,
        scratch_shapes=[pltpu.VMEM((planes, spread * mloc + 16, LANES), jnp.float32)],
        compiler_params=PARAMS,
        name="cut",
    )(view)
    bufs = [cuts[0]] + [
        permute(cuts[k], pairs_of(members, tiles, lambda m, t: (m ^ k, t))) for k in range(1, members)
    ]
    edge = jax.ShapeDtypeStruct((members * rows, LANES), jnp.bfloat16)
    send_even, send_odd = pl.pallas_call(
        functools.partial(edge_kernel, members),
        out_shape=[edge, edge],
        in_specs=[VMEM] * members,
        out_specs=[VMEM] * 2,
        compiler_params=PARAMS,
        name="edge",
    )(*bufs)
    got_even = permute(send_even, even_partner(members, tiles))
    got_odd = permute(send_odd, odd_partner(members, tiles))
    out = pl.pallas_call(
        functools.partial(count_kernel, members, mloc, width, step),
        out_shape=jax.ShapeDtypeStruct((planes, 26, step * LANES), jnp.float32),
        in_specs=[VMEM] * (members + 2),
        out_specs=VMEM,
        scratch_shapes=[pltpu.VMEM((planes + 2, members * rows, LANES), jnp.float32)],
        compiler_params=PARAMS,
        name="count",
    )(*bufs, got_even, got_odd)
    return out.transpose(1, 0, 2)


def solution(mesh):
    sizes = dict(mesh.shape)
    in_specs = (P("member", "tile", None),)
    out_specs = P(None, "tile", "member")
    body = functools.partial(local, sizes["member"], sizes["tile"])
    return jax.shard_map(body, mesh=mesh, in_specs=in_specs, out_specs=out_specs, check_vma=False)
```

```python
import functools

import jax
import jax.numpy as jnp
from jax import lax
from jax.experimental import pallas as pl
from jax.experimental.pallas import tpu as pltpu
from jax.sharding import PartitionSpec as P

NZ = 192
LANES = 128
EDGE = 2
LEAD = 8
PAD = 64.0
FAR = 4096.0
VMEM = pl.BlockSpec(memory_space=pltpu.VMEM)
ANY = pl.BlockSpec(memory_space=pl.ANY)
PARAMS = pltpu.CompilerParams(vmem_limit_bytes=8 << 20)


def permute(value, members, tiles, partner):
    pairs = []
    for m in range(members):
        for t in range(tiles):
            to_m, to_t = partner(m, t)
            pairs.append((m * tiles + t, to_m * tiles + to_t))
    return lax.ppermute(value, ("member", "tile"), pairs)


def beside(q, members, tiles, m, t):
    if m % 2 == 0:
        return m ^ (2 * q), t ^ 1
    if t == 0 or t == tiles - 1:
        return m ^ (2 * q if q else members // 2), t
    return m ^ (2 * q), (t + 1 if t % 2 else t - 1)


def edge_side():
    return (lax.axis_index("member") + lax.axis_index("tile")) % 2


def load_kernel(src, out):
    planes, rows = src.shape[0], src.shape[1]
    fill = jnp.full((planes, LEAD, LANES), PAD, jnp.float32)
    out[:, 0:LEAD, :] = fill
    out[:, LEAD : LEAD + rows, :] = src[...]
    out[:, LEAD + rows : LEAD + rows + LEAD, :] = fill


def spread_kernel(theirs, ours, both):
    core = lax.axis_index("member") % 2
    both[core] = ours[...]
    load_kernel(theirs, both.at[1 - core])


def window(both, mloc, p, start, size):
    base = start * mloc + LEAD - EDGE * mloc
    parts = [both[c, p, pl.ds(base + i, size, stride=mloc), :] for c in range(2) for i in range(mloc)]
    return jnp.concatenate(parts, axis=0).astype(jnp.bfloat16)


def edges_kernel(mloc, wide, step, theirs, ours, both, *edges):
    spread_kernel(theirs, ours, both)
    pair = lax.axis_index("member") // 2
    plane = (ours.shape[0] - 1) * (1 - edge_side())
    for q, edge in enumerate(edges):
        edge[...] = window(both, mloc, plane, (pair ^ q) * (2 * step), wide)


def blocks_kernel(mloc, width, step, both, *blocks):
    me = lax.axis_index("member")
    for q, block in enumerate(blocks):
        for p in range(block.shape[0]):
            block[p] = window(both, mloc, p, (me ^ (2 * q)) * step, width)


def join_kernel(*refs):
    bufs, out = refs[:-1], refs[-1]
    rows = bufs[0].shape[0]
    for k, buf in enumerate(bufs):
        out[k * rows : (k + 1) * rows, :] = buf[...]


def keys_of(stage, p, group, width, step, start):
    lane = lax.broadcasted_iota(jnp.int32, (8, LANES), 1)
    low, first, last = lane < 64, lane == 0, lane == LANES - 1
    at64, at63 = lane == 64, lane == 63
    base = group * 8 * width + start
    value = {
        j: stage[p, pl.ds(base + j, 8, stride=width), :] * 32.0
        for j in range(EDGE - 2, EDGE + step + 2)
    }
    keys = {}
    for j, here in value.items():
        before = pltpu.roll(here, 1, 1)
        after = pltpu.roll(here, LANES - 1, 1)
        phase = (j - EDGE) % 3
        if phase == 0:
            before = jnp.where(first, FAR, before)
        elif j - 1 in value:
            before = jnp.where(first, pltpu.roll(value[j - 1], 1, 1), before)
        if phase == 2:
            after = jnp.where(last, FAR, after)
        elif j + 1 in value:
            after = jnp.where(last, pltpu.roll(value[j + 1], LANES - 1, 1), after)
        if phase == 1:
            before = jnp.where(at64, FAR, before)
            after = jnp.where(at63, FAR, after)
        keys[j] = jnp.minimum(jnp.minimum(before, here + 1.0), after + 2.0)
    turned = {j: pltpu.roll(key, 64, 1) for j, key in keys.items()}
    row_before = {
        j: jnp.where(low, turned[j - 2], turned[j - 1]) for j in range(EDGE, EDGE + step + 3)
    }
    result = []
    for j in range(EDGE, EDGE + step):
        key = jnp.minimum(row_before[j], keys[j] + 3.0)
        result.append(jnp.minimum(key, row_before[j + 3] + 6.0))
    return result, [value[j] for j in range(EDGE, EDGE + step)]


def tally(best, value, out, p, j, add, total):
    sub = lax.broadcasted_iota(jnp.int32, (8, LANES), 0)
    code = best.astype(jnp.int32) & 31
    code = jnp.where(code > 13, code - 1, code)
    bit = jnp.where(best < value, jnp.int32(1) << ((code & 7) * 4), 0)
    kind = code >> 3
    for g in range(-(-out.shape[1] // 8)):
        word = jnp.where(kind == g, bit, 0)
        word = word + pltpu.roll(word, 4, 0)
        word = word + pltpu.roll(word, 2, 0)
        word = word + pltpu.roll(word, 1, 0)
        share = ((word >> (sub * 4)) & 15).astype(jnp.float32) * (1.0 / total)
        n = min(8, out.shape[1] - 8 * g)
        at = (p, slice(8 * g, 8 * g + n), slice(j * LANES, (j + 1) * LANES))
        out[at] = out[at] + share[:n] if add else share[:n]


def inner_kernel(width, step, total, *refs):
    blocks, (out, part, stage, tile_out, sem) = refs[:-5], refs[-5:]
    planes, rows = blocks[0].shape[0], blocks[0].shape[1]
    for q, block in enumerate(blocks):
        for p in range(planes):
            stage[p, q * rows : (q + 1) * rows, :] = block[p].astype(jnp.float32)
    for group in range(total // 8):
        layers = [keys_of(stage, p, group, width, step, 0) for p in range(planes)]
        for j in range(step):
            key = [layer[0][j] for layer in layers]
            value = [layer[1][j] for layer in layers]
            part[group, 0, j] = jnp.minimum(key[0] + 9.0, key[1] + 18.0)
            part[group, 1, j] = value[0]
            part[group, 2, j] = jnp.minimum(key[planes - 2], key[planes - 1] + 9.0)
            part[group, 3, j] = value[planes - 1]
            for p in range(1, planes - 1):
                best = jnp.minimum(jnp.minimum(key[p - 1], key[p] + 9.0), key[p + 1] + 18.0)
                tally(best, value[p], tile_out, p - 1, j, group > 0, total)
    copy = pltpu.make_async_copy(tile_out, out.at[pl.ds(1, planes - 2)], sem)
    copy.start()
    copy.wait()


def outer_kernel(wide, step, total, got, other, part, partial_out, out, stage, tile_out, sem):
    planes = out.shape[0]
    tile, tiles = lax.axis_index("tile"), lax.axis_size("tile")
    side = edge_side()
    start = (lax.axis_index("member") % 2) * step
    stage[1 - side] = got[...].astype(jnp.float32)
    stage[side] = other[...].astype(jnp.float32)

    @pl.when(tile == 0)
    def _():
        stage[0] = jnp.full(stage.shape[1:], PAD, jnp.float32)

    @pl.when(tile == tiles - 1)
    def _():
        stage[1] = jnp.full(stage.shape[1:], PAD, jnp.float32)

    for end, (plane, bias) in enumerate(((0, 0.0), (planes - 1, 18.0))):
        for group in range(total // 8):
            keys, _ = keys_of(stage, end, group, wide, step, start)
            for j in range(step):
                best = jnp.minimum(part[group, 2 * end, j], keys[j] + bias)
                tally(best, part[group, 2 * end + 1, j], tile_out, end, j, group > 0, total)
        pltpu.make_async_copy(tile_out.at[end], out.at[plane], sem.at[end]).start()
    for end, plane in enumerate((0, planes - 1)):
        pltpu.make_async_copy(tile_out.at[end], out.at[plane], sem.at[end]).wait()


def local(members, tiles, fields):
    mloc, planes, cols = fields.shape
    step = cols // members // LANES
    width, wide = step + 2 * EDGE, 2 * step + 2 * EDGE
    spread = cols // LANES
    assert LEAD >= EDGE * mloc
    total = members * mloc
    half = members // 2
    bf16, f32 = jnp.bfloat16, jnp.float32

    def swap(value):
        return permute(value, members, tiles, lambda m, t: (m ^ 1, t))

    view = fields.reshape(mloc, planes, spread, LANES).transpose(1, 2, 0, 3)
    view = view.reshape(planes, spread * mloc, LANES)
    padded = (planes, spread * mloc + 2 * LEAD, LANES)
    ours = pl.pallas_call(
        load_kernel,
        out_shape=jax.ShapeDtypeStruct(padded, f32),
        in_specs=[VMEM],
        out_specs=VMEM,
        compiler_params=PARAMS,
        name="load",
    )(view)
    both, *edges = pl.pallas_call(
        functools.partial(edges_kernel, mloc, wide, step),
        out_shape=[jax.ShapeDtypeStruct((2,) + padded, f32)]
        + [jax.ShapeDtypeStruct((2 * mloc * wide, LANES), bf16)] * half,
        in_specs=[VMEM] * 2,
        out_specs=[VMEM] * (half + 1),
        compiler_params=PARAMS,
        name="edges",
    )(swap(view), ours)
    blocks = pl.pallas_call(
        functools.partial(blocks_kernel, mloc, width, step),
        out_shape=[jax.ShapeDtypeStruct((planes, 2 * mloc * width, LANES), bf16)] * half,
        in_specs=[VMEM],
        out_specs=[VMEM] * half,
        compiler_params=PARAMS,
        cost_estimate=pl.CostEstimate(flops=1 << 24, bytes_accessed=1 << 24, transcendentals=0),
        name="blocks",
    )(both)
    got = [None] * half
    for q in list(range(1, half)) + [0]:
        got[q] = permute(edges[q], members, tiles, functools.partial(beside, q, members, tiles))
    blocks = [blocks[0]] + [
        permute(blocks[q], members, tiles, lambda m, t: (m ^ (2 * q), t)) for q in range(1, half)
    ]
    got = pl.pallas_call(
        join_kernel,
        out_shape=jax.ShapeDtypeStruct((total * wide, LANES), bf16),
        in_specs=[VMEM] * half,
        out_specs=VMEM,
        compiler_params=PARAMS,
        name="join",
    )(*got)
    other = swap(got)
    out_shape = jax.ShapeDtypeStruct((planes, 26, step * LANES), f32)
    part_shape = jax.ShapeDtypeStruct((total // 8, 4, step, 8, LANES), f32)
    out, part = pl.pallas_call(
        functools.partial(inner_kernel, width, step, total),
        out_shape=[out_shape, part_shape],
        in_specs=[VMEM] * half,
        out_specs=[ANY, VMEM],
        scratch_shapes=[
            pltpu.VMEM((planes, total * width, LANES), f32),
            pltpu.VMEM((planes - 2, 26, step * LANES), f32),
            pltpu.SemaphoreType.DMA,
        ],
        compiler_params=PARAMS,
        name="inner",
    )(*blocks)
    out = pl.pallas_call(
        functools.partial(outer_kernel, wide, step, total),
        out_shape=out_shape,
        in_specs=[VMEM, VMEM, VMEM, ANY],
        out_specs=ANY,
        scratch_shapes=[
            pltpu.VMEM((2, total * wide, LANES), f32),
            pltpu.VMEM((2, 26, step * LANES), f32),
            pltpu.SemaphoreType.DMA((2,)),
        ],
        input_output_aliases={3: 0},
        compiler_params=PARAMS,
        name="outer",
    )(got, other, part, out)
    return out.transpose(1, 0, 2)


def solution(mesh):
    sizes = dict(mesh.shape)
    in_specs = (P("member", "tile", None),)
    out_specs = P(None, "tile", "member")
    body = functools.partial(local, sizes["member"], sizes["tile"])
    return jax.shard_map(body, mesh=mesh, in_specs=in_specs, out_specs=out_specs, check_vma=False)
```

```python
import functools

import jax
import jax.numpy as jnp
from jax import lax
from jax.experimental import pallas as pl
from jax.experimental.pallas import tpu as pltpu
from jax.sharding import PartitionSpec as P

NZ = 192
LANES = 128
EDGE = 2
LEAD = 8
PAD = 64.0
FAR = 4096.0
VMEM = pl.BlockSpec(memory_space=pltpu.VMEM)
ANY = pl.BlockSpec(memory_space=pl.ANY)
PARAMS = pltpu.CompilerParams(vmem_limit_bytes=8 << 20)


def permute(value, members, tiles, partner):
    pairs = []
    for m in range(members):
        for t in range(tiles):
            to_m, to_t = partner(m, t)
            pairs.append((m * tiles + t, to_m * tiles + to_t))
    return lax.ppermute(value, ("member", "tile"), pairs)


def beside(q, members, tiles, m, t):
    if m % 2 == 0:
        return m ^ (2 * q), t ^ 1
    if t == 0 or t == tiles - 1:
        return m ^ (2 * q if q else members // 2), t
    return m ^ (2 * q), (t + 1 if t % 2 else t - 1)


def edge_side():
    return (lax.axis_index("member") + lax.axis_index("tile")) % 2


def load_kernel(src, out):
    planes, rows = src.shape[0], src.shape[1]
    fill = jnp.full((planes, LEAD, LANES), PAD, jnp.float32)
    out[:, 0:LEAD, :] = fill
    out[:, LEAD : LEAD + rows, :] = src[...]
    out[:, LEAD + rows : LEAD + rows + LEAD, :] = fill


def start_kernel(mloc, wide, step, src, ours, *sends):
    load_kernel(src, ours)
    pair = lax.axis_index("member") // 2
    for q, send in enumerate(sends):
        base = (pair ^ (q + 1)) * (2 * step * mloc) + LEAD - EDGE * mloc
        for p in range(src.shape[0]):
            parts = [ours[p, pl.ds(base + i, wide, stride=mloc), :] for i in range(mloc)]
            send[p] = jnp.concatenate(parts, axis=0).astype(jnp.bfloat16)


def spread_kernel(theirs, ours, both):
    core = lax.axis_index("member") % 2
    both[core] = ours[...]
    load_kernel(theirs, both.at[1 - core])


def window(both, mloc, p, start, size):
    base = start * mloc + LEAD - EDGE * mloc
    parts = [both[c, p, pl.ds(base + i, size, stride=mloc), :] for c in range(2) for i in range(mloc)]
    return jnp.concatenate(parts, axis=0).astype(jnp.bfloat16)


def edges_kernel(mloc, wide, step, theirs, ours, both, *edges):
    spread_kernel(theirs, ours, both)
    pair = lax.axis_index("member") // 2
    plane = (ours.shape[0] - 1) * (1 - edge_side())
    for q, edge in enumerate(edges):
        edge[...] = window(both, mloc, plane, (pair ^ q) * (2 * step), wide).astype(jnp.float32)


def block_kernel(mloc, width, step, both, block):
    start = lax.axis_index("member") * step
    for p in range(block.shape[0]):
        block[p] = window(both, mloc, p, start, width)


def cross_kernel(mloc, width, wide, step, *refs):
    n = len(refs) - 3
    raws, (keep, give, stage) = refs[:n], refs[n:]
    core = lax.axis_index("member") % 2
    for q, raw in enumerate(raws):
        stage[...] = raw[...].astype(jnp.float32)
        for dest, start in ((keep, core * step), (give, (1 - core) * step)):
            for p in range(raw.shape[0]):
                parts = [stage[p, pl.ds(i * wide + start, width), :] for i in range(mloc)]
                dest[q, p] = jnp.concatenate(parts, axis=0).astype(jnp.bfloat16)


def join_kernel(*refs):
    bufs, out = refs[:-1], refs[-1]
    rows = bufs[0].shape[0]
    for k, buf in enumerate(bufs):
        out[(len(bufs) - 1 - k) * rows : (len(bufs) - k) * rows, :] = buf[...].astype(out.dtype)


def keys_of(stage, p, group, width, step, start):
    lane = lax.broadcasted_iota(jnp.int32, (8, LANES), 1)
    low, first, last = lane < 64, lane == 0, lane == LANES - 1
    at64, at63 = lane == 64, lane == 63
    base = group * 8 * width + start
    value = {
        j: stage[p, pl.ds(base + j, 8, stride=width), :] * 32.0
        for j in range(EDGE - 2, EDGE + step + 2)
    }
    keys = {}
    for j, here in value.items():
        before = pltpu.roll(here, 1, 1)
        after = pltpu.roll(here, LANES - 1, 1)
        phase = (j - EDGE) % 3
        if phase == 0:
            before = jnp.where(first, FAR, before)
        elif j - 1 in value:
            before = jnp.where(first, pltpu.roll(value[j - 1], 1, 1), before)
        if phase == 2:
            after = jnp.where(last, FAR, after)
        elif j + 1 in value:
            after = jnp.where(last, pltpu.roll(value[j + 1], LANES - 1, 1), after)
        if phase == 1:
            before = jnp.where(at64, FAR, before)
            after = jnp.where(at63, FAR, after)
        keys[j] = jnp.minimum(jnp.minimum(before, here + 1.0), after + 2.0)
    turned = {j: pltpu.roll(key, 64, 1) for j, key in keys.items()}
    row_before = {
        j: jnp.where(low, turned[j - 2], turned[j - 1]) for j in range(EDGE, EDGE + step + 3)
    }
    result = []
    for j in range(EDGE, EDGE + step):
        key = jnp.minimum(row_before[j], keys[j] + 3.0)
        result.append(jnp.minimum(key, row_before[j + 3] + 6.0))
    return result, [value[j] for j in range(EDGE, EDGE + step)]


def tally(best, value, out, p, j, add, total):
    sub = lax.broadcasted_iota(jnp.int32, (8, LANES), 0)
    code = best.astype(jnp.int32) & 31
    code = jnp.where(code > 13, code - 1, code)
    bit = jnp.where(best < value, jnp.int32(1) << ((code & 7) * 4), 0)
    kind = code >> 3
    for g in range(-(-out.shape[1] // 8)):
        word = jnp.where(kind == g, bit, 0)
        word = word + pltpu.roll(word, 4, 0)
        word = word + pltpu.roll(word, 2, 0)
        word = word + pltpu.roll(word, 1, 0)
        share = ((word >> (sub * 4)) & 15).astype(jnp.float32) * (1.0 / total)
        n = min(8, out.shape[1] - 8 * g)
        at = (p, slice(8 * g, 8 * g + n), slice(j * LANES, (j + 1) * LANES))
        out[at] = out[at] + share[:n] if add else share[:n]


def inner_kernel(width, step, total, block, keep, came, out, part, stage, tile_out, sem):
    planes, rows = block.shape[0], block.shape[1]
    first = lax.axis_index("member") % 2 == 0
    for p in range(planes):
        stage[p, 0:rows, :] = block[p].astype(jnp.float32)
        for q in range(keep.shape[0]):
            here, there = keep[q, p].astype(jnp.float32), came[q, p].astype(jnp.float32)
            pairs = jnp.where(first, here, there), jnp.where(first, there, here)
            stage[p, (q + 1) * rows : (q + 2) * rows, :] = jnp.concatenate(pairs, axis=0)
    for group in range(total // 8):
        layers = [keys_of(stage, p, group, width, step, 0) for p in range(planes)]
        for j in range(step):
            key = [layer[0][j] for layer in layers]
            value = [layer[1][j] for layer in layers]
            part[group, 0, j] = jnp.minimum(key[0] + 9.0, key[1] + 18.0)
            part[group, 1, j] = value[0]
            part[group, 2, j] = jnp.minimum(key[planes - 2], key[planes - 1] + 9.0)
            part[group, 3, j] = value[planes - 1]
            for p in range(1, planes - 1):
                best = jnp.minimum(jnp.minimum(key[p - 1], key[p] + 9.0), key[p + 1] + 18.0)
                tally(best, value[p], tile_out, p - 1, j, group > 0, total)
    copy = pltpu.make_async_copy(tile_out, out.at[pl.ds(1, planes - 2)], sem)
    copy.start()
    copy.wait()


def outer_kernel(wide, step, total, got, other, part, partial_out, out, stage, tile_out, sem):
    planes = out.shape[0]
    tile, tiles = lax.axis_index("tile"), lax.axis_size("tile")
    side = edge_side()
    start = (lax.axis_index("member") % 2) * step
    stage[1 - side] = got[...].astype(jnp.float32)
    stage[side] = other[...].astype(jnp.float32)

    @pl.when(tile == 0)
    def _():
        stage[0] = jnp.full(stage.shape[1:], PAD, jnp.float32)

    @pl.when(tile == tiles - 1)
    def _():
        stage[1] = jnp.full(stage.shape[1:], PAD, jnp.float32)

    for end, (plane, bias) in enumerate(((0, 0.0), (planes - 1, 18.0))):
        for group in range(total // 8):
            keys, _ = keys_of(stage, end, group, wide, step, start)
            for j in range(step):
                best = jnp.minimum(part[group, 2 * end, j], keys[j] + bias)
                tally(best, part[group, 2 * end + 1, j], tile_out, end, j, group > 0, total)
        pltpu.make_async_copy(tile_out.at[end], out.at[plane], sem.at[end]).start()
    for end, plane in enumerate((0, planes - 1)):
        pltpu.make_async_copy(tile_out.at[end], out.at[plane], sem.at[end]).wait()


def local(members, tiles, fields):
    mloc, planes, cols = fields.shape
    step = cols // members // LANES
    width, wide = step + 2 * EDGE, 2 * step + 2 * EDGE
    spread = cols // LANES
    assert LEAD >= EDGE * mloc
    total = members * mloc
    half = members // 2
    bf16, f32 = jnp.bfloat16, jnp.float32

    def swap(value):
        return permute(value, members, tiles, lambda m, t: (m ^ 1, t))

    view = fields.reshape(mloc, planes, spread, LANES).transpose(1, 2, 0, 3)
    view = view.reshape(planes, spread * mloc, LANES)
    padded = (planes, spread * mloc + 2 * LEAD, LANES)
    ours, *sends = pl.pallas_call(
        functools.partial(start_kernel, mloc, wide, step),
        out_shape=[jax.ShapeDtypeStruct(padded, f32)]
        + [jax.ShapeDtypeStruct((planes, mloc * wide, LANES), bf16)] * (half - 1),
        in_specs=[VMEM],
        out_specs=[VMEM] * half,
        compiler_params=PARAMS,
        name="load",
    )(view)
    both, *edges = pl.pallas_call(
        functools.partial(edges_kernel, mloc, wide, step),
        out_shape=[jax.ShapeDtypeStruct((2,) + padded, f32)]
        + [jax.ShapeDtypeStruct((2 * mloc * wide, LANES), f32)] * half,
        in_specs=[VMEM] * 2,
        out_specs=[VMEM] * (half + 1),
        compiler_params=PARAMS,
        name="edges",
    )(swap(view), ours)
    raws = [permute(sends[q - 1], members, tiles, lambda m, t: (m ^ (2 * q), t)) for q in range(1, half)]
    *raws, both = lax.optimization_barrier((*raws, both))
    block = pl.pallas_call(
        functools.partial(block_kernel, mloc, width, step),
        out_shape=jax.ShapeDtypeStruct((planes, 2 * mloc * width, LANES), bf16),
        in_specs=[VMEM],
        out_specs=VMEM,
        compiler_params=PARAMS,
        name="block",
    )(both)
    kept = jax.ShapeDtypeStruct((half - 1, planes, mloc * width, LANES), bf16)
    keep, give = pl.pallas_call(
        functools.partial(cross_kernel, mloc, width, wide, step),
        out_shape=[kept, kept],
        in_specs=[VMEM] * (half - 1),
        out_specs=[VMEM] * 2,
        scratch_shapes=[pltpu.VMEM((planes, mloc * wide, LANES), f32)],
        compiler_params=PARAMS,
        name="cross",
    )(*raws)
    came = swap(give)
    got = [None] * half
    for q in list(range(1, half)) + [0]:
        got[q] = permute(edges[q], members, tiles, functools.partial(beside, q, members, tiles))
    out_shape = jax.ShapeDtypeStruct((planes, 26, step * LANES), f32)
    part_shape = jax.ShapeDtypeStruct((total // 8, 4, step, 8, LANES), f32)
    out, part = pl.pallas_call(
        functools.partial(inner_kernel, width, step, total),
        out_shape=[out_shape, part_shape],
        in_specs=[VMEM] * 3,
        out_specs=[ANY, VMEM],
        scratch_shapes=[
            pltpu.VMEM((planes, total * width, LANES), f32),
            pltpu.VMEM((planes - 2, 26, step * LANES), f32),
            pltpu.SemaphoreType.DMA,
        ],
        compiler_params=PARAMS,
        name="inner",
    )(block, keep, came)
    *got, part = lax.optimization_barrier((*got[::-1], part))
    got = got[::-1]
    got = pl.pallas_call(
        join_kernel,
        out_shape=jax.ShapeDtypeStruct((total * wide, LANES), bf16),
        in_specs=[VMEM] * half,
        out_specs=VMEM,
        compiler_params=PARAMS,
        name="join",
    )(*got[::-1])
    other = swap(got)
    out = pl.pallas_call(
        functools.partial(outer_kernel, wide, step, total),
        out_shape=out_shape,
        in_specs=[VMEM, VMEM, VMEM, ANY],
        out_specs=ANY,
        scratch_shapes=[
            pltpu.VMEM((2, total * wide, LANES), f32),
            pltpu.VMEM((2, 26, step * LANES), f32),
            pltpu.SemaphoreType.DMA((2,)),
        ],
        input_output_aliases={3: 0},
        compiler_params=PARAMS,
        name="outer",
    )(got, other, part, out)
    return out.transpose(1, 0, 2)


def solution(mesh):
    sizes = dict(mesh.shape)
    in_specs = (P("member", "tile", None),)
    out_specs = P(None, "tile", "member")
    body = functools.partial(local, sizes["member"], sizes["tile"])
    return jax.shard_map(body, mesh=mesh, in_specs=in_specs, out_specs=out_specs, check_vma=False)
```

```python
import functools

import jax
import jax.numpy as jnp
from jax import lax
from jax.experimental import pallas as pl
from jax.experimental.pallas import tpu as pltpu
from jax.sharding import PartitionSpec as P

NZ = 192
LANES = 128
EDGE = 2
LEAD = 8
PAD = 64.0
FAR = 4096.0
VMEM = pl.BlockSpec(memory_space=pltpu.VMEM)
ANY = pl.BlockSpec(memory_space=pl.ANY)
PARAMS = pltpu.CompilerParams(vmem_limit_bytes=8 << 20)


def permute(value, members, tiles, partner):
    pairs = []
    for m in range(members):
        for t in range(tiles):
            to_m, to_t = partner(m, t)
            pairs.append((m * tiles + t, to_m * tiles + to_t))
    return lax.ppermute(value, ("member", "tile"), pairs)


def beside(q, members, tiles, m, t):
    up = m % 2 == 0
    if t == (tiles - 1 if up else 0):
        return m ^ (2 * q if q else members // 2), t
    return m ^ (2 * q + 1), (t + 1 if up else t - 1)


def edge_side():
    return lax.axis_index("member") % 2


def load_kernel(src, out):
    planes, rows = src.shape[0], src.shape[1]
    fill = jnp.full((planes, LEAD, LANES), PAD, jnp.float32)
    out[:, 0:LEAD, :] = fill
    out[:, LEAD : LEAD + rows, :] = src[...]
    out[:, LEAD + rows : LEAD + rows + LEAD, :] = fill


def start_kernel(mloc, wide, step, src, ours, *sends):
    load_kernel(src, ours)
    pair = lax.axis_index("member") // 2
    for q, send in enumerate(sends):
        base = (pair ^ (q + 1)) * (2 * step * mloc) + LEAD - EDGE * mloc
        for p in range(src.shape[0]):
            parts = [ours[p, pl.ds(base + i, wide, stride=mloc), :] for i in range(mloc)]
            send[p] = jnp.concatenate(parts, axis=0).astype(jnp.bfloat16)


def spread_kernel(theirs, ours, both):
    core = lax.axis_index("member") % 2
    both[core] = ours[...]
    load_kernel(theirs, both.at[1 - core])


def window(both, mloc, p, start, size):
    base = start * mloc + LEAD - EDGE * mloc
    parts = [both[c, p, pl.ds(base + i, size, stride=mloc), :] for c in range(2) for i in range(mloc)]
    return jnp.concatenate(parts, axis=0).astype(jnp.bfloat16)


def edges_kernel(mloc, wide, step, theirs, ours, both, *edges):
    spread_kernel(theirs, ours, both)
    pair = lax.axis_index("member") // 2
    plane = (ours.shape[0] - 1) * (1 - edge_side())
    for q, edge in enumerate(edges):
        edge[...] = window(both, mloc, plane, (pair ^ q) * (2 * step), wide)


def block_kernel(mloc, width, step, both, block):
    start = lax.axis_index("member") * step
    for p in range(block.shape[0]):
        block[p] = window(both, mloc, p, start, width)


def cross_kernel(mloc, width, wide, step, *refs):
    n = len(refs) - 2 * mloc - 1
    raws, keeps, gives, stage = refs[:n], refs[n : n + mloc], refs[n + mloc : -1], refs[-1]
    core = lax.axis_index("member") % 2
    for q, raw in enumerate(raws):
        planes = raw.shape[0]
        stage[...] = raw[...].astype(jnp.float32)
        for dests, start in ((keeps, core * step), (gives, (1 - core) * step)):
            for i, dest in enumerate(dests):
                parts = [stage[p, pl.ds(i * wide + start, width), :] for p in range(planes)]
                dest[q] = jnp.concatenate(parts, axis=0).astype(jnp.bfloat16)


def join_kernel(*refs):
    bufs, out = refs[:-1], refs[-1]
    rows = bufs[0].shape[0]
    for k, buf in enumerate(bufs):
        out[(len(bufs) - 1 - k) * rows : (len(bufs) - k) * rows, :] = buf[...]


def keys_of(stage, p, group, width, step, start):
    lane = lax.broadcasted_iota(jnp.int32, (8, LANES), 1)
    low, first, last = lane < 64, lane == 0, lane == LANES - 1
    at64, at63 = lane == 64, lane == 63
    base = group * 8 * width + start
    value = {
        j: (stage if p is None else stage.at[p])[pl.ds(base + j, 8, stride=width), :] * 32.0
        for j in range(EDGE - 2, EDGE + step + 2)
    }
    keys = {}
    for j, here in value.items():
        before = pltpu.roll(here, 1, 1)
        after = pltpu.roll(here, LANES - 1, 1)
        phase = (j - EDGE) % 3
        if phase == 0:
            before = jnp.where(first, FAR, before)
        elif j - 1 in value:
            before = jnp.where(first, pltpu.roll(value[j - 1], 1, 1), before)
        if phase == 2:
            after = jnp.where(last, FAR, after)
        elif j + 1 in value:
            after = jnp.where(last, pltpu.roll(value[j + 1], LANES - 1, 1), after)
        if phase == 1:
            before = jnp.where(at64, FAR, before)
            after = jnp.where(at63, FAR, after)
        keys[j] = jnp.minimum(jnp.minimum(before, here + 1.0), after + 2.0)
    turned = {j: pltpu.roll(key, 64, 1) for j, key in keys.items()}
    row_before = {
        j: jnp.where(low, turned[j - 2], turned[j - 1]) for j in range(EDGE, EDGE + step + 3)
    }
    result = []
    for j in range(EDGE, EDGE + step):
        key = jnp.minimum(row_before[j], keys[j] + 3.0)
        result.append(jnp.minimum(key, row_before[j + 3] + 6.0))
    return result, [value[j] for j in range(EDGE, EDGE + step)]


def tally(best, value, out, p, j, add, total):
    sub = lax.broadcasted_iota(jnp.int32, (8, LANES), 0)
    code = best.astype(jnp.int32) & 31
    code = jnp.where(code > 13, code - 1, code)
    bit = jnp.where(best < value, jnp.int32(1) << ((code & 7) * 4), 0)
    kind = code >> 3
    for g in range(-(-out.shape[1] // 8)):
        word = jnp.where(kind == g, bit, 0)
        word = word + pltpu.roll(word, 4, 0)
        word = word + pltpu.roll(word, 2, 0)
        word = word + pltpu.roll(word, 1, 0)
        share = ((word >> (sub * 4)) & 15).astype(jnp.float32) * (1.0 / total)
        n = min(8, out.shape[1] - 8 * g)
        at = (p, slice(8 * g, 8 * g + n), slice(j * LANES, (j + 1) * LANES))
        out[at] = out[at] + share[:n] if add else share[:n]


def inner_kernel(mloc, width, step, total, block, *refs):
    keeps, cames, (tile_out, part, stage) = refs[:mloc], refs[mloc : 2 * mloc], refs[2 * mloc :]
    planes, rows = block.shape[0], block.shape[1]
    first = lax.axis_index("member") % 2 == 1
    for p in range(planes):
        stage[p, 0:rows, :] = block[p].astype(jnp.float32)
    for q in range(keeps[0].shape[0]):
        here = [keep[q].astype(jnp.float32) for keep in keeps]
        there = [came[q].astype(jnp.float32) for came in cames]
        both = [jnp.where(first, a, b) for a, b in zip(here, there)]
        both += [jnp.where(first, b, a) for a, b in zip(here, there)]
        for p in range(planes):
            parts = [value[p * width : (p + 1) * width] for value in both]
            stage[p, (q + 1) * rows : (q + 2) * rows, :] = jnp.concatenate(parts, axis=0)
    for group in range(total // 8):
        layers = []
        for p in range(planes):
            layers.append(keys_of(stage, p, group, width, step, 0))
            if p == 1:
                for j in range(step):
                    part[group, 0, j] = jnp.minimum(layers[0][0][j] + 9.0, layers[1][0][j] + 18.0)
                    part[group, 1, j] = layers[0][1][j]
            if p < 2:
                continue
            for j in range(step):
                best = jnp.minimum(layers[p - 2][0][j], layers[p - 1][0][j] + 9.0)
                best = jnp.minimum(best, layers[p][0][j] + 18.0)
                tally(best, layers[p - 1][1][j], tile_out, p - 2, j, group > 0, total)
        for j in range(step):
            part[group, 2, j] = jnp.minimum(layers[-2][0][j], layers[-1][0][j] + 9.0)
            part[group, 3, j] = layers[-1][1][j]


def half_kernel(wide, step, total, other, halo, part, source, out, stage, tile_out, sem):
    planes = out.shape[0]
    tile, tiles = lax.axis_index("tile"), lax.axis_size("tile")
    end = edge_side() if other else 1 - edge_side()
    start = (lax.axis_index("member") % 2) * step
    bias = end.astype(jnp.float32) * 18.0
    copies = []
    if not other:
        copies.append(pltpu.make_async_copy(source, out.at[pl.ds(1, planes - 2)], sem.at[0]))
        copies[0].start()
    stage[...] = halo[...].astype(jnp.float32)

    @pl.when(tile == end * (tiles - 1))
    def _():
        stage[...] = jnp.full(stage.shape, PAD, jnp.float32)

    for group in range(total // 8):
        keys, _ = keys_of(stage, None, group, wide, step, start)
        for j in range(step):
            best = jnp.minimum(part[group, 2 * end, j], keys[j] + bias)
            tally(best, part[group, 2 * end + 1, j], tile_out, 0, j, group > 0, total)
    copies.append(pltpu.make_async_copy(tile_out.at[0], out.at[end * (planes - 1)], sem.at[1]))
    copies[-1].start()
    for copy in copies:
        copy.wait()


def local(members, tiles, fields):
    mloc, planes, cols = fields.shape
    step = cols // members // LANES
    width, wide = step + 2 * EDGE, 2 * step + 2 * EDGE
    spread = cols // LANES
    assert LEAD >= EDGE * mloc
    total = members * mloc
    half = members // 2
    bf16, f32 = jnp.bfloat16, jnp.float32

    def swap(value):
        return permute(value, members, tiles, lambda m, t: (m ^ 1, t))

    view = fields.reshape(mloc, planes, spread, LANES).transpose(1, 2, 0, 3)
    view = view.reshape(planes, spread * mloc, LANES)
    padded = (planes, spread * mloc + 2 * LEAD, LANES)
    ours, *sends = pl.pallas_call(
        functools.partial(start_kernel, mloc, wide, step),
        out_shape=[jax.ShapeDtypeStruct(padded, f32)]
        + [jax.ShapeDtypeStruct((planes, mloc * wide, LANES), bf16)] * (half - 1),
        in_specs=[VMEM],
        out_specs=[VMEM] * half,
        compiler_params=PARAMS,
        name="load",
    )(view)
    both, *edges = pl.pallas_call(
        functools.partial(edges_kernel, mloc, wide, step),
        out_shape=[jax.ShapeDtypeStruct((2,) + padded, f32)]
        + [jax.ShapeDtypeStruct((2 * mloc * wide, LANES), bf16)] * half,
        in_specs=[VMEM] * 2,
        out_specs=[VMEM] * (half + 1),
        compiler_params=PARAMS,
        name="edges",
    )(swap(view), ours)
    raws = [permute(sends[q - 1], members, tiles, lambda m, t: (m ^ (2 * q + 1), t)) for q in range(1, half)]
    *raws, both = lax.optimization_barrier((*raws, both))
    block = pl.pallas_call(
        functools.partial(block_kernel, mloc, width, step),
        out_shape=jax.ShapeDtypeStruct((planes, 2 * mloc * width, LANES), bf16),
        in_specs=[VMEM],
        out_specs=VMEM,
        compiler_params=PARAMS,
        name="block",
    )(both)
    kept = jax.ShapeDtypeStruct((half - 1, planes * width, LANES), bf16)
    crossed = pl.pallas_call(
        functools.partial(cross_kernel, mloc, width, wide, step),
        out_shape=[kept] * (2 * mloc),
        in_specs=[VMEM] * (half - 1),
        out_specs=[VMEM] * (2 * mloc),
        scratch_shapes=[pltpu.VMEM((planes, mloc * wide, LANES), f32)],
        compiler_params=PARAMS,
        name="cross",
    )(*raws)
    keeps, cames = crossed[:mloc], [swap(give) for give in crossed[mloc:]]
    got = [None] * half
    for q in list(range(1, half)) + [0]:
        got[q] = permute(edges[q], members, tiles, functools.partial(beside, q, members, tiles))
    out_shape = jax.ShapeDtypeStruct((planes, 26, step * LANES), f32)
    part_shape = jax.ShapeDtypeStruct((total // 8, 4, step, 8, LANES), f32)
    inner, part = pl.pallas_call(
        functools.partial(inner_kernel, mloc, width, step, total),
        out_shape=[jax.ShapeDtypeStruct((planes - 2, 26, step * LANES), f32), part_shape],
        in_specs=[VMEM] * (1 + 2 * mloc),
        out_specs=[VMEM, VMEM],
        scratch_shapes=[pltpu.VMEM((planes, total * width, LANES), f32)],
        compiler_params=PARAMS,
        name="inner",
    )(block, *keeps, *cames)
    *got, part = lax.optimization_barrier((*got[::-1], part))
    got = got[::-1]
    got = pl.pallas_call(
        join_kernel,
        out_shape=jax.ShapeDtypeStruct((total * wide, LANES), bf16),
        in_specs=[VMEM] * half,
        out_specs=VMEM,
        compiler_params=PARAMS,
        name="join",
    )(*got[::-1])
    other = swap(got)
    out = inner
    for other, halo in enumerate((got, other)):
        out = pl.pallas_call(
            functools.partial(half_kernel, wide, step, total, other),
            out_shape=out_shape,
            in_specs=[VMEM, VMEM, ANY if other else VMEM],
            out_specs=ANY,
            scratch_shapes=[
                pltpu.VMEM((total * wide, LANES), f32),
                pltpu.VMEM((1, 26, step * LANES), f32),
                pltpu.SemaphoreType.DMA((2,)),
            ],
            input_output_aliases={2: 0} if other else {},
            compiler_params=PARAMS,
            name="outer",
        )(halo, part, out)
    return out.transpose(1, 0, 2)


def solution(mesh):
    sizes = dict(mesh.shape)
    in_specs = (P("member", "tile", None),)
    out_specs = P(None, "tile", "member")
    body = functools.partial(local, sizes["member"], sizes["tile"])
    return jax.shard_map(body, mesh=mesh, in_specs=in_specs, out_specs=out_specs, check_vma=False)
```

```python
import functools

import jax
import jax.numpy as jnp
from jax import lax
from jax.experimental import pallas as pl
from jax.experimental.pallas import tpu as pltpu
from jax.sharding import PartitionSpec as P

NZ = 192
LANES = 128
EDGE = 2
LEAD = 8
PAD = 64.0
FAR = 4096.0
VMEM = pl.BlockSpec(memory_space=pltpu.VMEM)
ANY = pl.BlockSpec(memory_space=pl.ANY)
PARAMS = pltpu.CompilerParams(vmem_limit_bytes=8 << 20)


def permute(value, members, tiles, partner):
    pairs = []
    for m in range(members):
        for t in range(tiles):
            to_m, to_t = partner(m, t)
            pairs.append((m * tiles + t, to_m * tiles + to_t))
    return lax.ppermute(value, ("member", "tile"), pairs)


def beside(q, members, tiles, m, t):
    up = m % 2 == 0
    if t == (tiles - 1 if up else 0):
        return m ^ (2 * q if q else members // 2), t
    return m ^ (2 * q + 1), (t + 1 if up else t - 1)


def edge_side():
    return lax.axis_index("member") % 2


def load_kernel(src, out):
    planes, rows = src.shape[0], src.shape[1]
    fill = jnp.full((planes, LEAD, LANES), PAD, jnp.float32)
    out[:, 0:LEAD, :] = fill
    out[:, LEAD : LEAD + rows, :] = src[...]
    out[:, LEAD + rows : LEAD + rows + LEAD, :] = fill


def mark_kernel(out):
    out[...] = jnp.full(out.shape, PAD, out.dtype)


def start_kernel(mloc, wide, step, src, early, ours, *sends):
    load_kernel(src, ours)
    ours[0, 0:LEAD, :] = early[...]
    pair = lax.axis_index("member") // 2
    for q, send in enumerate(sends):
        base = (pair ^ (q + 1)) * (2 * step * mloc) + LEAD - EDGE * mloc
        for p in range(src.shape[0]):
            parts = [ours[p, pl.ds(base + i, wide, stride=mloc), :] for i in range(mloc)]
            send[p] = jnp.concatenate(parts, axis=0).astype(jnp.bfloat16)


def spread_kernel(theirs, ours, both):
    core = lax.axis_index("member") % 2
    both[core] = ours[...]
    load_kernel(theirs, both.at[1 - core])


def window(both, mloc, p, start, size):
    base = start * mloc + LEAD - EDGE * mloc
    parts = [both[c, p, pl.ds(base + i, size, stride=mloc), :] for c in range(2) for i in range(mloc)]
    return jnp.concatenate(parts, axis=0).astype(jnp.bfloat16)


def edges_kernel(mloc, wide, step, theirs, ours, both, *edges):
    spread_kernel(theirs, ours, both)
    pair = lax.axis_index("member") // 2
    plane = (ours.shape[0] - 1) * (1 - edge_side())
    for q, edge in enumerate(edges):
        edge[...] = window(both, mloc, plane, (pair ^ q) * (2 * step), wide)


def block_kernel(mloc, width, step, both, block):
    start = lax.axis_index("member") * step
    for p in range(block.shape[0]):
        block[p] = window(both, mloc, p, start, width)


def cross_kernel(mloc, width, wide, step, *refs):
    n = len(refs) - 2 * mloc - 1
    raws, keeps, gives, stage = refs[:n], refs[n : n + mloc], refs[n + mloc : -1], refs[-1]
    core = lax.axis_index("member") % 2
    for q, raw in enumerate(raws):
        planes = raw.shape[0]
        stage[...] = raw[...].astype(jnp.float32)
        for dests, start in ((keeps, core * step), (gives, (1 - core) * step)):
            for i, dest in enumerate(dests):
                parts = [stage[p, pl.ds(i * wide + start, width), :] for p in range(planes)]
                dest[q] = jnp.concatenate(parts, axis=0).astype(jnp.bfloat16)


def join_kernel(*refs):
    bufs, out = refs[:-1], refs[-1]
    rows = bufs[0].shape[0]
    for k, buf in enumerate(bufs):
        out[(len(bufs) - 1 - k) * rows : (len(bufs) - k) * rows, :] = buf[...]


def keys_of(stage, p, group, width, step, start):
    lane = lax.broadcasted_iota(jnp.int32, (8, LANES), 1)
    low, first, last = lane < 64, lane == 0, lane == LANES - 1
    at64, at63 = lane == 64, lane == 63
    base = group * 8 * width + start
    value = {
        j: (stage if p is None else stage.at[p])[pl.ds(base + j, 8, stride=width), :] * 32.0
        for j in range(EDGE - 2, EDGE + step + 2)
    }
    keys = {}
    for j, here in value.items():
        before = pltpu.roll(here, 1, 1)
        after = pltpu.roll(here, LANES - 1, 1)
        phase = (j - EDGE) % 3
        if phase == 0:
            before = jnp.where(first, FAR, before)
        elif j - 1 in value:
            before = jnp.where(first, pltpu.roll(value[j - 1], 1, 1), before)
        if phase == 2:
            after = jnp.where(last, FAR, after)
        elif j + 1 in value:
            after = jnp.where(last, pltpu.roll(value[j + 1], LANES - 1, 1), after)
        if phase == 1:
            before = jnp.where(at64, FAR, before)
            after = jnp.where(at63, FAR, after)
        keys[j] = jnp.minimum(jnp.minimum(before, here + 1.0), after + 2.0)
    turned = {j: pltpu.roll(key, 64, 1) for j, key in keys.items()}
    row_before = {
        j: jnp.where(low, turned[j - 2], turned[j - 1]) for j in range(EDGE, EDGE + step + 3)
    }
    result = []
    for j in range(EDGE, EDGE + step):
        key = jnp.minimum(row_before[j], keys[j] + 3.0)
        result.append(jnp.minimum(key, row_before[j + 3] + 6.0))
    return result, [value[j] for j in range(EDGE, EDGE + step)]


def tally(best, value, out, p, j, add, total):
    sub = lax.broadcasted_iota(jnp.int32, (8, LANES), 0)
    code = best.astype(jnp.int32) & 31
    code = jnp.where(code > 13, code - 1, code)
    bit = jnp.where(best < value, jnp.int32(1) << ((code & 7) * 4), 0)
    kind = code >> 3
    for g in range(-(-out.shape[1] // 8)):
        word = jnp.where(kind == g, bit, 0)
        word = word + pltpu.roll(word, 4, 0)
        word = word + pltpu.roll(word, 2, 0)
        word = word + pltpu.roll(word, 1, 0)
        share = ((word >> (sub * 4)) & 15).astype(jnp.float32) * (1.0 / total)
        n = min(8, out.shape[1] - 8 * g)
        at = (p, slice(8 * g, 8 * g + n), slice(j * LANES, (j + 1) * LANES))
        out[at] = out[at] + share[:n] if add else share[:n]


def inner_kernel(mloc, width, step, total, block, *refs):
    keeps, cames, (tile_out, part, stage) = refs[:mloc], refs[mloc : 2 * mloc], refs[2 * mloc :]
    planes, rows = block.shape[0], block.shape[1]
    first = lax.axis_index("member") % 2 == 1
    for p in range(planes):
        stage[p, 0:rows, :] = block[p].astype(jnp.float32)
    for q in range(keeps[0].shape[0]):
        here = [keep[q].astype(jnp.float32) for keep in keeps]
        there = [came[q].astype(jnp.float32) for came in cames]
        both = [jnp.where(first, a, b) for a, b in zip(here, there)]
        both += [jnp.where(first, b, a) for a, b in zip(here, there)]
        for p in range(planes):
            parts = [value[p * width : (p + 1) * width] for value in both]
            stage[p, (q + 1) * rows : (q + 2) * rows, :] = jnp.concatenate(parts, axis=0)
    for group in range(total // 8):
        layers = []
        for p in range(planes):
            layers.append(keys_of(stage, p, group, width, step, 0))
            if p == 1:
                for j in range(step):
                    part[group, 0, j] = jnp.minimum(layers[0][0][j] + 9.0, layers[1][0][j] + 18.0)
                    part[group, 1, j] = layers[0][1][j]
            if p < 2:
                continue
            for j in range(step):
                best = jnp.minimum(layers[p - 2][0][j], layers[p - 1][0][j] + 9.0)
                best = jnp.minimum(best, layers[p][0][j] + 18.0)
                tally(best, layers[p - 1][1][j], tile_out, p - 2, j, group > 0, total)
        for j in range(step):
            part[group, 2, j] = jnp.minimum(layers[-2][0][j], layers[-1][0][j] + 9.0)
            part[group, 3, j] = layers[-1][1][j]


def half_kernel(wide, step, total, other, halo, part, source, out, stage, tile_out, sem):
    planes = out.shape[0]
    tile, tiles = lax.axis_index("tile"), lax.axis_size("tile")
    end = edge_side() if other else 1 - edge_side()
    start = (lax.axis_index("member") % 2) * step
    bias = end.astype(jnp.float32) * 18.0
    copies = []
    if not other:
        copies.append(pltpu.make_async_copy(source, out.at[pl.ds(1, planes - 2)], sem.at[0]))
        copies[0].start()
    stage[...] = halo[...].astype(jnp.float32)

    @pl.when(tile == end * (tiles - 1))
    def _():
        stage[...] = jnp.full(stage.shape, PAD, jnp.float32)

    for group in range(total // 8):
        keys, _ = keys_of(stage, None, group, wide, step, start)
        for j in range(step):
            best = jnp.minimum(part[group, 2 * end, j], keys[j] + bias)
            tally(best, part[group, 2 * end + 1, j], tile_out, 0, j, group > 0, total)
    copies.append(pltpu.make_async_copy(tile_out.at[0], out.at[end * (planes - 1)], sem.at[1]))
    copies[-1].start()
    for copy in copies:
        copy.wait()


def local(members, tiles, fields):
    mloc, planes, cols = fields.shape
    step = cols // members // LANES
    width, wide = step + 2 * EDGE, 2 * step + 2 * EDGE
    spread = cols // LANES
    assert LEAD >= EDGE * mloc
    total = members * mloc
    half = members // 2
    bf16, f32 = jnp.bfloat16, jnp.float32

    def swap(value):
        return permute(value, members, tiles, lambda m, t: (m ^ 1, t))

    view = fields.reshape(mloc, planes, spread, LANES).transpose(1, 2, 0, 3)
    view = view.reshape(planes, spread * mloc, LANES)
    padded = (planes, spread * mloc + 2 * LEAD, LANES)
    early = pl.pallas_call(
        mark_kernel,
        out_shape=jax.ShapeDtypeStruct((8, LANES), f32),
        out_specs=VMEM,
        compiler_params=PARAMS,
        cost_estimate=pl.CostEstimate(flops=1 << 36, bytes_accessed=1 << 24, transcendentals=0),
        name="mark",
    )()
    ours, *sends = pl.pallas_call(
        functools.partial(start_kernel, mloc, wide, step),
        out_shape=[jax.ShapeDtypeStruct(padded, f32)]
        + [jax.ShapeDtypeStruct((planes, mloc * wide, LANES), bf16)] * (half - 1),
        in_specs=[VMEM, VMEM],
        out_specs=[VMEM] * half,
        compiler_params=PARAMS,
        name="load",
    )(view, early)
    both, *edges = pl.pallas_call(
        functools.partial(edges_kernel, mloc, wide, step),
        out_shape=[jax.ShapeDtypeStruct((2,) + padded, f32)]
        + [jax.ShapeDtypeStruct((2 * mloc * wide, LANES), bf16)] * half,
        in_specs=[VMEM] * 2,
        out_specs=[VMEM] * (half + 1),
        compiler_params=PARAMS,
        name="edges",
    )(swap(view), ours)
    raws = [permute(sends[q - 1], members, tiles, lambda m, t: (m ^ (2 * q + 1), t)) for q in range(1, half)]
    *raws, both = lax.optimization_barrier((*raws, both))
    block = pl.pallas_call(
        functools.partial(block_kernel, mloc, width, step),
        out_shape=jax.ShapeDtypeStruct((planes, 2 * mloc * width, LANES), bf16),
        in_specs=[VMEM],
        out_specs=VMEM,
        compiler_params=PARAMS,
        name="block",
    )(both)
    kept = jax.ShapeDtypeStruct((half - 1, planes * width, LANES), bf16)
    crossed = pl.pallas_call(
        functools.partial(cross_kernel, mloc, width, wide, step),
        out_shape=[kept] * (2 * mloc),
        in_specs=[VMEM] * (half - 1),
        out_specs=[VMEM] * (2 * mloc),
        scratch_shapes=[pltpu.VMEM((planes, mloc * wide, LANES), f32)],
        compiler_params=PARAMS,
        name="cross",
    )(*raws)
    keeps, cames = crossed[:mloc], [swap(give) for give in crossed[mloc:]]
    got = [None] * half
    for q in list(range(1, half)) + [0]:
        got[q] = permute(edges[q], members, tiles, functools.partial(beside, q, members, tiles))
    out_shape = jax.ShapeDtypeStruct((planes, 26, step * LANES), f32)
    part_shape = jax.ShapeDtypeStruct((total // 8, 4, step, 8, LANES), f32)
    inner, part = pl.pallas_call(
        functools.partial(inner_kernel, mloc, width, step, total),
        out_shape=[jax.ShapeDtypeStruct((planes - 2, 26, step * LANES), f32), part_shape],
        in_specs=[VMEM] * (1 + 2 * mloc),
        out_specs=[VMEM, VMEM],
        scratch_shapes=[pltpu.VMEM((planes, total * width, LANES), f32)],
        compiler_params=PARAMS,
        name="inner",
    )(block, *keeps, *cames)
    *got, part = lax.optimization_barrier((*got[::-1], part))
    got = got[::-1]
    got = pl.pallas_call(
        join_kernel,
        out_shape=jax.ShapeDtypeStruct((total * wide, LANES), bf16),
        in_specs=[VMEM] * half,
        out_specs=VMEM,
        compiler_params=PARAMS,
        name="join",
    )(*got[::-1])
    other = swap(got)
    out = inner
    for other, halo in enumerate((got, other)):
        out = pl.pallas_call(
            functools.partial(half_kernel, wide, step, total, other),
            out_shape=out_shape,
            in_specs=[VMEM, VMEM, ANY if other else VMEM],
            out_specs=ANY,
            scratch_shapes=[
                pltpu.VMEM((total * wide, LANES), f32),
                pltpu.VMEM((1, 26, step * LANES), f32),
                pltpu.SemaphoreType.DMA((2,)),
            ],
            input_output_aliases={2: 0} if other else {},
            compiler_params=PARAMS,
            name="outer",
        )(halo, part, out)
    return out.transpose(1, 0, 2)


def solution(mesh):
    sizes = dict(mesh.shape)
    in_specs = (P("member", "tile", None),)
    out_specs = P(None, "tile", "member")
    body = functools.partial(local, sizes["member"], sizes["tile"])
    return jax.shard_map(body, mesh=mesh, in_specs=in_specs, out_specs=out_specs, check_vma=False)
```

```python
import functools

import jax
import jax.numpy as jnp
from jax import lax
from jax.experimental import pallas as pl
from jax.experimental.pallas import tpu as pltpu
from jax.sharding import PartitionSpec as P

NZ = 192
LANES = 128
EDGE = 2
LEAD = 8
PAD = 64.0
FAR = 4096.0
VMEM = pl.BlockSpec(memory_space=pltpu.VMEM)
ANY = pl.BlockSpec(memory_space=pl.ANY)
PARAMS = pltpu.CompilerParams(vmem_limit_bytes=8 << 20)


def permute(value, members, tiles, partner):
    pairs = []
    for m in range(members):
        for t in range(tiles):
            to_m, to_t = partner(m, t)
            pairs.append((m * tiles + t, to_m * tiles + to_t))
    return lax.ppermute(value, ("member", "tile"), pairs)


def beside(q, members, tiles, m, t):
    ends, near, swap = (0, tiles - 1), t ^ 1, m ^ (2 * q)
    if t in ends:
        if (m % 2 == 0) == (q == 0):
            return swap & ~1, near
        return m ^ (2 * q if q else members // 2), t
    if m % 2 == 0:
        return (swap | 1 if q and near in ends else swap), near
    return swap, (t + 1 if t % 2 else t - 1)


def place():
    core, tile, tiles = lax.axis_index("member") % 2, lax.axis_index("tile"), lax.axis_size("tile")
    last = jnp.logical_or(tile == 0, tile == tiles - 1)
    inside = (core + tile + 1) % 2
    return core, last, jnp.where(last, (tile == 0).astype(jnp.int32), inside)


def load_kernel(src, out):
    planes, rows = src.shape[0], src.shape[1]
    fill = jnp.full((planes, LEAD, LANES), PAD, jnp.float32)
    out[:, 0:LEAD, :] = fill
    out[:, LEAD : LEAD + rows, :] = src[...]
    out[:, LEAD + rows : LEAD + rows + LEAD, :] = fill


def mark_kernel(out):
    out[...] = jnp.full(out.shape, PAD, out.dtype)


def start_kernel(mloc, wide, step, src, early, ours, *sends):
    load_kernel(src, ours)
    ours[0, 0:LEAD, :] = early[...]
    pair = lax.axis_index("member") // 2
    for q, send in enumerate(sends):
        base = (pair ^ (q + 1)) * (2 * step * mloc) + LEAD - EDGE * mloc
        for p in range(src.shape[0]):
            parts = [ours[p, pl.ds(base + i, wide, stride=mloc), :] for i in range(mloc)]
            send[p] = jnp.concatenate(parts, axis=0).astype(jnp.bfloat16)


def spread_kernel(theirs, ours, both):
    core = lax.axis_index("member") % 2
    both[core] = ours[...]
    load_kernel(theirs, both.at[1 - core])


def window(both, mloc, p, start, size):
    base = start * mloc + LEAD - EDGE * mloc
    parts = [both[c, p, pl.ds(base + i, size, stride=mloc), :] for c in range(2) for i in range(mloc)]
    return jnp.concatenate(parts, axis=0).astype(jnp.bfloat16)


def edges_kernel(mloc, wide, step, theirs, ours, both, *edges):
    spread_kernel(theirs, ours, both)
    pair = lax.axis_index("member") // 2
    plane = (ours.shape[0] - 1) * place()[2]
    for q, edge in enumerate(edges):
        edge[...] = window(both, mloc, plane, (pair ^ q) * (2 * step), wide)


def block_kernel(mloc, width, step, both, block):
    start = lax.axis_index("member") * step
    for p in range(block.shape[0]):
        block[p] = window(both, mloc, p, start, width)


def cross_kernel(mloc, width, wide, step, *refs):
    n = len(refs) - 2 * mloc - 1
    raws, keeps, gives, stage = refs[:n], refs[n : n + mloc], refs[n + mloc : -1], refs[-1]
    core = lax.axis_index("member") % 2
    for q, raw in enumerate(raws):
        planes = raw.shape[0]
        stage[...] = raw[...].astype(jnp.float32)
        for dests, start in ((keeps, core * step), (gives, (1 - core) * step)):
            for i, dest in enumerate(dests):
                parts = [stage[p, pl.ds(i * wide + start, width), :] for p in range(planes)]
                dest[q] = jnp.concatenate(parts, axis=0).astype(jnp.bfloat16)


def join_kernel(*refs):
    bufs, out = refs[:-1], refs[-1]
    rows = bufs[0].shape[0]
    for k, buf in enumerate(bufs):
        out[(len(bufs) - 1 - k) * rows : (len(bufs) - k) * rows, :] = buf[...]


def keys_of(stage, p, group, width, step, start):
    lane = lax.broadcasted_iota(jnp.int32, (8, LANES), 1)
    low, first, last = lane < 64, lane == 0, lane == LANES - 1
    at64, at63 = lane == 64, lane == 63
    base = group * 8 * width + start
    value = {
        j: (stage if p is None else stage.at[p])[pl.ds(base + j, 8, stride=width), :] * 32.0
        for j in range(EDGE - 2, EDGE + step + 2)
    }
    keys = {}
    for j, here in value.items():
        before = pltpu.roll(here, 1, 1)
        after = pltpu.roll(here, LANES - 1, 1)
        phase = (j - EDGE) % 3
        if phase == 0:
            before = jnp.where(first, FAR, before)
        elif j - 1 in value:
            before = jnp.where(first, pltpu.roll(value[j - 1], 1, 1), before)
        if phase == 2:
            after = jnp.where(last, FAR, after)
        elif j + 1 in value:
            after = jnp.where(last, pltpu.roll(value[j + 1], LANES - 1, 1), after)
        if phase == 1:
            before = jnp.where(at64, FAR, before)
            after = jnp.where(at63, FAR, after)
        keys[j] = jnp.minimum(jnp.minimum(before, here + 1.0), after + 2.0)
    turned = {j: pltpu.roll(key, 64, 1) for j, key in keys.items()}
    row_before = {
        j: jnp.where(low, turned[j - 2], turned[j - 1]) for j in range(EDGE, EDGE + step + 3)
    }
    result = []
    for j in range(EDGE, EDGE + step):
        key = jnp.minimum(row_before[j], keys[j] + 3.0)
        result.append(jnp.minimum(key, row_before[j + 3] + 6.0))
    return result, [value[j] for j in range(EDGE, EDGE + step)]


def tally(best, value, out, p, j, add, total):
    sub = lax.broadcasted_iota(jnp.int32, (8, LANES), 0)
    code = best.astype(jnp.int32) & 31
    code = jnp.where(code > 13, code - 1, code)
    bit = jnp.where(best < value, jnp.int32(1) << ((code & 7) * 4), 0)
    kind = code >> 3
    for g in range(-(-out.shape[1] // 8)):
        word = jnp.where(kind == g, bit, 0)
        word = word + pltpu.roll(word, 4, 0)
        word = word + pltpu.roll(word, 2, 0)
        word = word + pltpu.roll(word, 1, 0)
        share = ((word >> (sub * 4)) & 15).astype(jnp.float32) * (1.0 / total)
        n = min(8, out.shape[1] - 8 * g)
        at = (p, slice(8 * g, 8 * g + n), slice(j * LANES, (j + 1) * LANES))
        out[at] = out[at] + share[:n] if add else share[:n]


def inner_kernel(mloc, width, step, total, block, *refs):
    keeps, cames, (tile_out, part, stage) = refs[:mloc], refs[mloc : 2 * mloc], refs[2 * mloc :]
    planes, rows = block.shape[0], block.shape[1]
    first = lax.axis_index("member") % 2 == 1
    for p in range(planes):
        stage[p, 0:rows, :] = block[p].astype(jnp.float32)
    for q in range(keeps[0].shape[0]):
        here = [keep[q].astype(jnp.float32) for keep in keeps]
        there = [came[q].astype(jnp.float32) for came in cames]
        both = [jnp.where(first, a, b) for a, b in zip(here, there)]
        both += [jnp.where(first, b, a) for a, b in zip(here, there)]
        for p in range(planes):
            parts = [value[p * width : (p + 1) * width] for value in both]
            stage[p, (q + 1) * rows : (q + 2) * rows, :] = jnp.concatenate(parts, axis=0)
    for group in range(total // 8):
        layers = []
        for p in range(planes):
            layers.append(keys_of(stage, p, group, width, step, 0))
            if p == 1:
                for j in range(step):
                    part[group, 0, j] = jnp.minimum(layers[0][0][j] + 9.0, layers[1][0][j] + 18.0)
                    part[group, 1, j] = layers[0][1][j]
            if p < 2:
                continue
            for j in range(step):
                best = jnp.minimum(layers[p - 2][0][j], layers[p - 1][0][j] + 9.0)
                best = jnp.minimum(best, layers[p][0][j] + 18.0)
                tally(best, layers[p - 1][1][j], tile_out, p - 2, j, group > 0, total)
        for j in range(step):
            part[group, 2, j] = jnp.minimum(layers[-2][0][j], layers[-1][0][j] + 9.0)
            part[group, 3, j] = layers[-1][1][j]


def half_kernel(wide, step, total, own, *refs):
    *halos, part, source, out, stage, tile_out, sem = refs
    planes = out.shape[0]
    core, last, toward = place()
    later = len(halos) == 2
    end = jnp.where(last, toward, 1 - toward) if later else jnp.where(last, 1 - toward, toward)
    start = core * step
    bias = end.astype(jnp.float32) * 18.0
    copies = []
    if later:
        got, other = halos
        stage[...] = other[...].astype(jnp.float32)
        for rows, owner in ((slice(0, own), 0), (slice(own, got.shape[0]), 1)):

            @pl.when(jnp.logical_and(last, core == owner))
            def _():
                stage[rows, :] = got[rows, :].astype(jnp.float32)
    else:
        copies.append(pltpu.make_async_copy(source, out.at[pl.ds(1, planes - 2)], sem.at[0]))
        copies[0].start()
        stage[...] = halos[0][...].astype(jnp.float32)

        @pl.when(last)
        def _():
            stage[...] = jnp.full(stage.shape, PAD, jnp.float32)

    for group in range(total // 8):
        keys, _ = keys_of(stage, None, group, wide, step, start)
        for j in range(step):
            best = jnp.minimum(part[group, 2 * end, j], keys[j] + bias)
            tally(best, part[group, 2 * end + 1, j], tile_out, 0, j, group > 0, total)
    copies.append(pltpu.make_async_copy(tile_out.at[0], out.at[end * (planes - 1)], sem.at[1]))
    copies[-1].start()
    for copy in copies:
        copy.wait()


def local(members, tiles, fields):
    mloc, planes, cols = fields.shape
    step = cols // members // LANES
    width, wide = step + 2 * EDGE, 2 * step + 2 * EDGE
    spread = cols // LANES
    assert LEAD >= EDGE * mloc
    total = members * mloc
    half = members // 2
    bf16, f32 = jnp.bfloat16, jnp.float32

    def swap(value):
        return permute(value, members, tiles, lambda m, t: (m ^ 1, t))

    view = fields.reshape(mloc, planes, spread, LANES).transpose(1, 2, 0, 3)
    view = view.reshape(planes, spread * mloc, LANES)
    padded = (planes, spread * mloc + 2 * LEAD, LANES)
    early = pl.pallas_call(
        mark_kernel,
        out_shape=jax.ShapeDtypeStruct((8, LANES), f32),
        out_specs=VMEM,
        compiler_params=PARAMS,
        cost_estimate=pl.CostEstimate(flops=1 << 36, bytes_accessed=1 << 24, transcendentals=0),
        name="mark",
    )()
    ours, *sends = pl.pallas_call(
        functools.partial(start_kernel, mloc, wide, step),
        out_shape=[jax.ShapeDtypeStruct(padded, f32)]
        + [jax.ShapeDtypeStruct((planes, mloc * wide, LANES), bf16)] * (half - 1),
        in_specs=[VMEM, VMEM],
        out_specs=[VMEM] * half,
        compiler_params=PARAMS,
        name="load",
    )(view, early)
    both, *edges = pl.pallas_call(
        functools.partial(edges_kernel, mloc, wide, step),
        out_shape=[jax.ShapeDtypeStruct((2,) + padded, f32)]
        + [jax.ShapeDtypeStruct((2 * mloc * wide, LANES), bf16)] * half,
        in_specs=[VMEM] * 2,
        out_specs=[VMEM] * (half + 1),
        compiler_params=PARAMS,
        name="edges",
    )(swap(view), ours)
    raws = [permute(sends[q - 1], members, tiles, lambda m, t: (m ^ (2 * q + 1), t)) for q in range(1, half)]
    *raws, both = lax.optimization_barrier((*raws, both))
    block = pl.pallas_call(
        functools.partial(block_kernel, mloc, width, step),
        out_shape=jax.ShapeDtypeStruct((planes, 2 * mloc * width, LANES), bf16),
        in_specs=[VMEM],
        out_specs=VMEM,
        compiler_params=PARAMS,
        name="block",
    )(both)
    kept = jax.ShapeDtypeStruct((half - 1, planes * width, LANES), bf16)
    crossed = pl.pallas_call(
        functools.partial(cross_kernel, mloc, width, wide, step),
        out_shape=[kept] * (2 * mloc),
        in_specs=[VMEM] * (half - 1),
        out_specs=[VMEM] * (2 * mloc),
        scratch_shapes=[pltpu.VMEM((planes, mloc * wide, LANES), f32)],
        compiler_params=PARAMS,
        name="cross",
    )(*raws)
    keeps, cames = crossed[:mloc], [swap(give) for give in crossed[mloc:]]
    got = [None] * half
    for q in list(range(1, half)) + [0]:
        got[q] = permute(edges[q], members, tiles, functools.partial(beside, q, members, tiles))
    out_shape = jax.ShapeDtypeStruct((planes, 26, step * LANES), f32)
    part_shape = jax.ShapeDtypeStruct((total // 8, 4, step, 8, LANES), f32)
    inner, part = pl.pallas_call(
        functools.partial(inner_kernel, mloc, width, step, total),
        out_shape=[jax.ShapeDtypeStruct((planes - 2, 26, step * LANES), f32), part_shape],
        in_specs=[VMEM] * (1 + 2 * mloc),
        out_specs=[VMEM, VMEM],
        scratch_shapes=[pltpu.VMEM((planes, total * width, LANES), f32)],
        compiler_params=PARAMS,
        name="inner",
    )(block, *keeps, *cames)
    *got, part = lax.optimization_barrier((*got[::-1], part))
    got = got[::-1]
    got = pl.pallas_call(
        join_kernel,
        out_shape=jax.ShapeDtypeStruct((total * wide, LANES), bf16),
        in_specs=[VMEM] * half,
        out_specs=VMEM,
        compiler_params=PARAMS,
        name="join",
    )(*got[::-1])
    other = swap(got)
    out = inner
    for halos in ((got,), (got, other)):
        later = len(halos) == 2
        out = pl.pallas_call(
            functools.partial(half_kernel, wide, step, total, 2 * mloc * wide),
            out_shape=out_shape,
            in_specs=[VMEM] * (len(halos) + 1) + [ANY if later else VMEM],
            out_specs=ANY,
            scratch_shapes=[
                pltpu.VMEM((total * wide, LANES), f32),
                pltpu.VMEM((1, 26, step * LANES), f32),
                pltpu.SemaphoreType.DMA((2,)),
            ],
            input_output_aliases={3: 0} if later else {},
            compiler_params=PARAMS,
            name="outer",
        )(*halos, part, out)
    return out.transpose(1, 0, 2)


def solution(mesh):
    sizes = dict(mesh.shape)
    in_specs = (P("member", "tile", None),)
    out_specs = P(None, "tile", "member")
    body = functools.partial(local, sizes["member"], sizes["tile"])
    return jax.shard_map(body, mesh=mesh, in_specs=in_specs, out_specs=out_specs, check_vma=False)
```

```python
import functools

import jax
import jax.numpy as jnp
from jax import lax
from jax.experimental import pallas as pl
from jax.experimental.pallas import tpu as pltpu
from jax.sharding import PartitionSpec as P

NZ = 192
LANES = 128
EDGE = 2
LEAD = 8
PAD = 64.0
FAR = 4096.0
VMEM = pl.BlockSpec(memory_space=pltpu.VMEM)
ANY = pl.BlockSpec(memory_space=pl.ANY)
PARAMS = pltpu.CompilerParams(vmem_limit_bytes=8 << 20)


def permute(value, members, tiles, partner):
    pairs = []
    for m in range(members):
        for t in range(tiles):
            to_m, to_t = partner(m, t)
            pairs.append((m * tiles + t, to_m * tiles + to_t))
    return lax.ppermute(value, ("member", "tile"), pairs)


def beside(q, members, tiles, m, t):
    ends, near, swap = (0, tiles - 1), t ^ 1, m ^ (2 * q)
    if t in ends:
        if (m % 2 == 0) == (q == 0):
            return swap & ~1, near
        return m ^ (2 * q if q else members // 2), t
    if m % 2 == 0:
        return (swap | 1 if q and near in ends else swap), near
    return swap, (t + 1 if t % 2 else t - 1)


def place():
    core, tile, tiles = lax.axis_index("member") % 2, lax.axis_index("tile"), lax.axis_size("tile")
    last = jnp.logical_or(tile == 0, tile == tiles - 1)
    inside = (core + tile + 1) % 2
    return core, last, jnp.where(last, (tile == 0).astype(jnp.int32), inside)


def load_kernel(src, out):
    planes, rows = src.shape[0], src.shape[1]
    fill = jnp.full((planes, LEAD, LANES), PAD, jnp.float32)
    out[:, 0:LEAD, :] = fill
    out[:, LEAD : LEAD + rows, :] = src[...]
    out[:, LEAD + rows : LEAD + rows + LEAD, :] = fill


def mark_kernel(out):
    out[...] = jnp.full(out.shape, PAD, out.dtype)


def start_kernel(mloc, wide, step, src, early, ours, *sends):
    load_kernel(src, ours)
    ours[0, 0:LEAD, :] = early[...]
    pair = lax.axis_index("member") // 2
    for q, send in enumerate(sends):
        base = (pair ^ (q + 1)) * (2 * step * mloc) + LEAD - EDGE * mloc
        for p in range(src.shape[0]):
            parts = [ours[p, pl.ds(base + i, wide, stride=mloc), :] for i in range(mloc)]
            send[p] = jnp.concatenate(parts, axis=0).astype(jnp.bfloat16)


def spread_kernel(theirs, ours, both):
    core = lax.axis_index("member") % 2
    both[core] = ours[...]
    load_kernel(theirs, both.at[1 - core])


def window(both, mloc, p, start, size):
    base = start * mloc + LEAD - EDGE * mloc
    parts = [both[c, p, pl.ds(base + i, size, stride=mloc), :] for c in range(2) for i in range(mloc)]
    return jnp.concatenate(parts, axis=0).astype(jnp.bfloat16)


def edges_kernel(mloc, wide, step, theirs, ours, rim, *refs):
    edges, both = refs[:-1], refs[-1]
    core = lax.axis_index("member") % 2
    pair = lax.axis_index("member") // 2
    plane = (ours.shape[0] - 1) * place()[2]
    rows = theirs.shape[1]
    fill = jnp.full((LEAD, LANES), PAD, jnp.float32)
    rim[...] = fill
    both[core, 0] = ours[plane]
    both[1 - core, 0, 0:LEAD, :] = fill
    both[1 - core, 0, LEAD : LEAD + rows, :] = theirs[plane]
    both[1 - core, 0, LEAD + rows : LEAD + rows + LEAD, :] = fill
    for q, edge in enumerate(edges):
        edge[...] = window(both, mloc, 0, (pair ^ q) * (2 * step), wide)


def block_kernel(mloc, width, step, theirs, ours, rim, block, both):
    spread_kernel(theirs, ours, both)
    both[0, 0, 0:LEAD, :] = rim[...]
    start = lax.axis_index("member") * step
    for p in range(block.shape[0]):
        block[p] = window(both, mloc, p, start, width)


def cross_kernel(mloc, width, wide, step, *refs):
    n = len(refs) - 2 * mloc - 1
    raws, keeps, gives, stage = refs[:n], refs[n : n + mloc], refs[n + mloc : -1], refs[-1]
    core = lax.axis_index("member") % 2
    for q, raw in enumerate(raws):
        planes = raw.shape[0]
        stage[...] = raw[...].astype(jnp.float32)
        for dests, start in ((keeps, core * step), (gives, (1 - core) * step)):
            for i, dest in enumerate(dests):
                parts = [stage[p, pl.ds(i * wide + start, width), :] for p in range(planes)]
                dest[q] = jnp.concatenate(parts, axis=0).astype(jnp.bfloat16)


def join_kernel(*refs):
    bufs, out = refs[:-1], refs[-1]
    rows = bufs[0].shape[0]
    for k, buf in enumerate(bufs):
        out[(len(bufs) - 1 - k) * rows : (len(bufs) - k) * rows, :] = buf[...]


def keys_of(stage, p, group, width, step, start):
    lane = lax.broadcasted_iota(jnp.int32, (8, LANES), 1)
    low, first, last = lane < 64, lane == 0, lane == LANES - 1
    at64, at63 = lane == 64, lane == 63
    base = group * 8 * width + start
    value = {
        j: (stage if p is None else stage.at[p])[pl.ds(base + j, 8, stride=width), :] * 32.0
        for j in range(EDGE - 2, EDGE + step + 2)
    }
    keys = {}
    for j, here in value.items():
        before = pltpu.roll(here, 1, 1)
        after = pltpu.roll(here, LANES - 1, 1)
        phase = (j - EDGE) % 3
        if phase == 0:
            before = jnp.where(first, FAR, before)
        elif j - 1 in value:
            before = jnp.where(first, pltpu.roll(value[j - 1], 1, 1), before)
        if phase == 2:
            after = jnp.where(last, FAR, after)
        elif j + 1 in value:
            after = jnp.where(last, pltpu.roll(value[j + 1], LANES - 1, 1), after)
        if phase == 1:
            before = jnp.where(at64, FAR, before)
            after = jnp.where(at63, FAR, after)
        keys[j] = jnp.minimum(jnp.minimum(before, here + 1.0), after + 2.0)
    turned = {j: pltpu.roll(key, 64, 1) for j, key in keys.items()}
    row_before = {
        j: jnp.where(low, turned[j - 2], turned[j - 1]) for j in range(EDGE, EDGE + step + 3)
    }
    result = []
    for j in range(EDGE, EDGE + step):
        key = jnp.minimum(row_before[j], keys[j] + 3.0)
        result.append(jnp.minimum(key, row_before[j + 3] + 6.0))
    return result, [value[j] for j in range(EDGE, EDGE + step)]


def tally(best, value, out, p, j, add, total):
    sub = lax.broadcasted_iota(jnp.int32, (8, LANES), 0)
    code = best.astype(jnp.int32) & 31
    code = jnp.where(code > 13, code - 1, code)
    bit = jnp.where(best < value, jnp.int32(1) << ((code & 7) * 4), 0)
    kind = code >> 3
    for g in range(-(-out.shape[1] // 8)):
        word = jnp.where(kind == g, bit, 0)
        word = word + pltpu.roll(word, 4, 0)
        word = word + pltpu.roll(word, 2, 0)
        word = word + pltpu.roll(word, 1, 0)
        share = ((word >> (sub * 4)) & 15).astype(jnp.float32) * (1.0 / total)
        n = min(8, out.shape[1] - 8 * g)
        at = (p, slice(8 * g, 8 * g + n), slice(j * LANES, (j + 1) * LANES))
        out[at] = out[at] + share[:n] if add else share[:n]


def inner_kernel(mloc, width, step, total, block, *refs):
    keeps, cames, (tile_out, part, stage) = refs[:mloc], refs[mloc : 2 * mloc], refs[2 * mloc :]
    planes, rows = block.shape[0], block.shape[1]
    first = lax.axis_index("member") % 2 == 1
    for p in range(planes):
        stage[p, 0:rows, :] = block[p].astype(jnp.float32)
    for q in range(keeps[0].shape[0]):
        here = [keep[q].astype(jnp.float32) for keep in keeps]
        there = [came[q].astype(jnp.float32) for came in cames]
        both = [jnp.where(first, a, b) for a, b in zip(here, there)]
        both += [jnp.where(first, b, a) for a, b in zip(here, there)]
        for p in range(planes):
            parts = [value[p * width : (p + 1) * width] for value in both]
            stage[p, (q + 1) * rows : (q + 2) * rows, :] = jnp.concatenate(parts, axis=0)
    for group in range(total // 8):
        layers = []
        for p in range(planes):
            layers.append(keys_of(stage, p, group, width, step, 0))
            if p == 1:
                for j in range(step):
                    part[group, 0, j] = jnp.minimum(layers[0][0][j] + 9.0, layers[1][0][j] + 18.0)
                    part[group, 1, j] = layers[0][1][j]
            if p < 2:
                continue
            for j in range(step):
                best = jnp.minimum(layers[p - 2][0][j], layers[p - 1][0][j] + 9.0)
                best = jnp.minimum(best, layers[p][0][j] + 18.0)
                tally(best, layers[p - 1][1][j], tile_out, p - 2, j, group > 0, total)
        for j in range(step):
            part[group, 2, j] = jnp.minimum(layers[-2][0][j], layers[-1][0][j] + 9.0)
            part[group, 3, j] = layers[-1][1][j]


def half_kernel(wide, step, total, own, *refs):
    *halos, part, source, out, stage, tile_out, sem = refs
    planes = out.shape[0]
    core, last, toward = place()
    later = len(halos) == 2
    end = jnp.where(last, toward, 1 - toward) if later else jnp.where(last, 1 - toward, toward)
    start = core * step
    bias = end.astype(jnp.float32) * 18.0
    copies = []
    if later:
        got, other = halos
        stage[...] = other[...].astype(jnp.float32)
        for rows, owner in ((slice(0, own), 0), (slice(own, got.shape[0]), 1)):

            @pl.when(jnp.logical_and(last, core == owner))
            def _():
                stage[rows, :] = got[rows, :].astype(jnp.float32)
    else:
        copies.append(pltpu.make_async_copy(source, out.at[pl.ds(1, planes - 2)], sem.at[0]))
        copies[0].start()
        stage[...] = halos[0][...].astype(jnp.float32)

        @pl.when(last)
        def _():
            stage[...] = jnp.full(stage.shape, PAD, jnp.float32)

    for group in range(total // 8):
        keys, _ = keys_of(stage, None, group, wide, step, start)
        for j in range(step):
            best = jnp.minimum(part[group, 2 * end, j], keys[j] + bias)
            tally(best, part[group, 2 * end + 1, j], tile_out, 0, j, group > 0, total)
    copies.append(pltpu.make_async_copy(tile_out.at[0], out.at[end * (planes - 1)], sem.at[1]))
    copies[-1].start()
    for copy in copies:
        copy.wait()


def local(members, tiles, fields):
    mloc, planes, cols = fields.shape
    step = cols // members // LANES
    width, wide = step + 2 * EDGE, 2 * step + 2 * EDGE
    spread = cols // LANES
    assert LEAD >= EDGE * mloc
    total = members * mloc
    half = members // 2
    bf16, f32 = jnp.bfloat16, jnp.float32

    def swap(value):
        return permute(value, members, tiles, lambda m, t: (m ^ 1, t))

    view = fields.reshape(mloc, planes, spread, LANES).transpose(1, 2, 0, 3)
    view = view.reshape(planes, spread * mloc, LANES)
    padded = (planes, spread * mloc + 2 * LEAD, LANES)
    early = pl.pallas_call(
        mark_kernel,
        out_shape=jax.ShapeDtypeStruct((8, LANES), f32),
        out_specs=VMEM,
        compiler_params=PARAMS,
        cost_estimate=pl.CostEstimate(flops=1 << 36, bytes_accessed=1 << 24, transcendentals=0),
        name="mark",
    )()
    ours, *sends = pl.pallas_call(
        functools.partial(start_kernel, mloc, wide, step),
        out_shape=[jax.ShapeDtypeStruct(padded, f32)]
        + [jax.ShapeDtypeStruct((planes, mloc * wide, LANES), bf16)] * (half - 1),
        in_specs=[VMEM, VMEM],
        out_specs=[VMEM] * half,
        compiler_params=PARAMS,
        name="load",
    )(view, early)
    theirs = swap(view)
    rim, *edges = pl.pallas_call(
        functools.partial(edges_kernel, mloc, wide, step),
        out_shape=[jax.ShapeDtypeStruct((LEAD, LANES), f32)]
        + [jax.ShapeDtypeStruct((2 * mloc * wide, LANES), bf16)] * half,
        in_specs=[VMEM] * 2,
        out_specs=[VMEM] * (half + 1),
        scratch_shapes=[pltpu.VMEM((2, 1) + padded[1:], f32)],
        compiler_params=PARAMS,
        name="edges",
    )(theirs, ours)
    raws = [permute(sends[q - 1], members, tiles, lambda m, t: (m ^ (2 * q + 1), t)) for q in range(1, half)]
    *raws, rim = lax.optimization_barrier((*raws, rim))
    block = pl.pallas_call(
        functools.partial(block_kernel, mloc, width, step),
        out_shape=jax.ShapeDtypeStruct((planes, 2 * mloc * width, LANES), bf16),
        in_specs=[VMEM] * 3,
        out_specs=VMEM,
        scratch_shapes=[pltpu.VMEM((2,) + padded, f32)],
        compiler_params=PARAMS,
        name="block",
    )(theirs, ours, rim)
    kept = jax.ShapeDtypeStruct((half - 1, planes * width, LANES), bf16)
    crossed = pl.pallas_call(
        functools.partial(cross_kernel, mloc, width, wide, step),
        out_shape=[kept] * (2 * mloc),
        in_specs=[VMEM] * (half - 1),
        out_specs=[VMEM] * (2 * mloc),
        scratch_shapes=[pltpu.VMEM((planes, mloc * wide, LANES), f32)],
        compiler_params=PARAMS,
        name="cross",
    )(*raws)
    keeps, cames = crossed[:mloc], [swap(give) for give in crossed[mloc:]]
    got = [None] * half
    for q in list(range(1, half)) + [0]:
        got[q] = permute(edges[q], members, tiles, functools.partial(beside, q, members, tiles))
    out_shape = jax.ShapeDtypeStruct((planes, 26, step * LANES), f32)
    part_shape = jax.ShapeDtypeStruct((total // 8, 4, step, 8, LANES), f32)
    inner, part = pl.pallas_call(
        functools.partial(inner_kernel, mloc, width, step, total),
        out_shape=[jax.ShapeDtypeStruct((planes - 2, 26, step * LANES), f32), part_shape],
        in_specs=[VMEM] * (1 + 2 * mloc),
        out_specs=[VMEM, VMEM],
        scratch_shapes=[pltpu.VMEM((planes, total * width, LANES), f32)],
        compiler_params=PARAMS,
        name="inner",
    )(block, *keeps, *cames)
    *got, part = lax.optimization_barrier((*got[::-1], part))
    got = got[::-1]
    got = pl.pallas_call(
        join_kernel,
        out_shape=jax.ShapeDtypeStruct((total * wide, LANES), bf16),
        in_specs=[VMEM] * half,
        out_specs=VMEM,
        compiler_params=PARAMS,
        name="join",
    )(*got[::-1])
    other = swap(got)
    out = inner
    for halos in ((got,), (got, other)):
        later = len(halos) == 2
        out = pl.pallas_call(
            functools.partial(half_kernel, wide, step, total, 2 * mloc * wide),
            out_shape=out_shape,
            in_specs=[VMEM] * (len(halos) + 1) + [ANY if later else VMEM],
            out_specs=ANY,
            scratch_shapes=[
                pltpu.VMEM((total * wide, LANES), f32),
                pltpu.VMEM((1, 26, step * LANES), f32),
                pltpu.SemaphoreType.DMA((2,)),
            ],
            input_output_aliases={3: 0} if later else {},
            compiler_params=PARAMS,
            name="outer",
        )(*halos, part, out)
    return out.transpose(1, 0, 2)


def solution(mesh):
    sizes = dict(mesh.shape)
    in_specs = (P("member", "tile", None),)
    out_specs = P(None, "tile", "member")
    body = functools.partial(local, sizes["member"], sizes["tile"])
    return jax.shard_map(body, mesh=mesh, in_specs=in_specs, out_specs=out_specs, check_vma=False)
```

```python
import functools

import jax
import jax.numpy as jnp
from jax import lax
from jax.experimental import pallas as pl
from jax.experimental.pallas import tpu as pltpu
from jax.sharding import PartitionSpec as P

NZ = 192
LANES = 128
EDGE = 2
LEAD = 8
PAD = 64.0
FAR = 4096.0
VMEM = pl.BlockSpec(memory_space=pltpu.VMEM)
ANY = pl.BlockSpec(memory_space=pl.ANY)
PARAMS = pltpu.CompilerParams(vmem_limit_bytes=8 << 20)


def permute(value, members, tiles, partner):
    pairs = []
    for m in range(members):
        for t in range(tiles):
            to_m, to_t = partner(m, t)
            pairs.append((m * tiles + t, to_m * tiles + to_t))
    return lax.ppermute(value, ("member", "tile"), pairs)


def beside(q, members, tiles, m, t):
    ends, near, swap = (0, tiles - 1), t ^ 1, m ^ (2 * q)
    if t in ends:
        if (m % 2 == 0) == (q == 0):
            return swap & ~1, near
        return m ^ (2 * q if q else members // 2), t
    if m % 2 == 0:
        return (swap | 1 if q and near in ends else swap), near
    return swap, (t + 1 if t % 2 else t - 1)


def place():
    core, tile, tiles = lax.axis_index("member") % 2, lax.axis_index("tile"), lax.axis_size("tile")
    last = jnp.logical_or(tile == 0, tile == tiles - 1)
    inside = (core + tile + 1) % 2
    return core, last, jnp.where(last, (tile == 0).astype(jnp.int32), inside)


def load_kernel(src, out):
    planes, rows = src.shape[0], src.shape[1]
    fill = jnp.full((planes, LEAD, LANES), PAD, jnp.float32)
    out[:, 0:LEAD, :] = fill
    out[:, LEAD : LEAD + rows, :] = src[...]
    out[:, LEAD + rows : LEAD + rows + LEAD, :] = fill


def mark_kernel(out):
    out[...] = jnp.full(out.shape, PAD, out.dtype)


def start_kernel(mloc, wide, step, src, early, ours, *sends):
    load_kernel(src, ours)
    ours[0, 0:LEAD, :] = early[...]
    pair = lax.axis_index("member") // 2
    for q, send in enumerate(sends):
        base = (pair ^ (q + 1)) * (2 * step * mloc) + LEAD - EDGE * mloc
        for p in range(src.shape[0]):
            parts = [ours[p, pl.ds(base + i, wide, stride=mloc), :] for i in range(mloc)]
            send[p] = jnp.concatenate(parts, axis=0).astype(jnp.bfloat16)


def spread_kernel(theirs, ours, both):
    core = lax.axis_index("member") % 2
    both[core] = ours[...]
    load_kernel(theirs, both.at[1 - core])


def window(both, mloc, p, start, size):
    base = start * mloc + LEAD - EDGE * mloc
    parts = [both[c, p, pl.ds(base + i, size, stride=mloc), :] for c in range(2) for i in range(mloc)]
    return jnp.concatenate(parts, axis=0).astype(jnp.bfloat16)


def edges_kernel(mloc, wide, step, theirs, ours, rim, *refs):
    edges, both = refs[:-1], refs[-1]
    core = lax.axis_index("member") % 2
    pair = lax.axis_index("member") // 2
    plane = (ours.shape[0] - 1) * place()[2]
    rows = theirs.shape[1]
    fill = jnp.full((LEAD, LANES), PAD, jnp.float32)
    rim[...] = fill
    both[core, 0] = ours[plane]
    both[1 - core, 0, 0:LEAD, :] = fill
    both[1 - core, 0, LEAD : LEAD + rows, :] = theirs[plane]
    both[1 - core, 0, LEAD + rows : LEAD + rows + LEAD, :] = fill
    for q, edge in enumerate(edges):
        edge[...] = window(both, mloc, 0, (pair ^ q) * (2 * step), wide)


def block_kernel(mloc, width, step, theirs, ours, rim, block, both):
    spread_kernel(theirs, ours, both)
    both[0, 0, 0:LEAD, :] = rim[...]
    start = lax.axis_index("member") * step
    for p in range(block.shape[0]):
        block[p] = window(both, mloc, p, start, width)


def cross_kernel(mloc, width, wide, step, *refs):
    n = len(refs) - 2 * mloc - 1
    raws, keeps, gives, stage = refs[:n], refs[n : n + mloc], refs[n + mloc : -1], refs[-1]
    core = lax.axis_index("member") % 2
    for q, raw in enumerate(raws):
        planes = raw.shape[0]
        stage[...] = raw[...].astype(jnp.float32)
        for dests, start in ((keeps, core * step), (gives, (1 - core) * step)):
            for i, dest in enumerate(dests):
                parts = [stage[p, pl.ds(i * wide + start, width), :] for p in range(planes)]
                dest[q] = jnp.concatenate(parts, axis=0).astype(jnp.bfloat16)


def join_kernel(*refs):
    bufs, out = refs[:-1], refs[-1]
    rows = bufs[0].shape[0]
    for k, buf in enumerate(bufs):
        out[(len(bufs) - 1 - k) * rows : (len(bufs) - k) * rows, :] = buf[...]


def keys_of(stage, p, group, width, step, start):
    lane = lax.broadcasted_iota(jnp.int32, (8, LANES), 1)
    low, first, last = lane < 64, lane == 0, lane == LANES - 1
    at64, at63 = lane == 64, lane == 63
    base = group * 8 * width + start
    value = {
        j: (stage if p is None else stage.at[p])[pl.ds(base + j, 8, stride=width), :] * 32.0
        for j in range(EDGE - 2, EDGE + step + 2)
    }
    keys = {}
    for j, here in value.items():
        before = pltpu.roll(here, 1, 1)
        after = pltpu.roll(here, LANES - 1, 1)
        phase = (j - EDGE) % 3
        if phase == 0:
            before = jnp.where(first, FAR, before)
        elif j - 1 in value:
            before = jnp.where(first, pltpu.roll(value[j - 1], 1, 1), before)
        if phase == 2:
            after = jnp.where(last, FAR, after)
        elif j + 1 in value:
            after = jnp.where(last, pltpu.roll(value[j + 1], LANES - 1, 1), after)
        if phase == 1:
            before = jnp.where(at64, FAR, before)
            after = jnp.where(at63, FAR, after)
        keys[j] = jnp.minimum(jnp.minimum(before, here + 1.0), after + 2.0)
    turned = {j: pltpu.roll(key, 64, 1) for j, key in keys.items()}
    row_before = {
        j: jnp.where(low, turned[j - 2], turned[j - 1]) for j in range(EDGE, EDGE + step + 3)
    }
    result = []
    for j in range(EDGE, EDGE + step):
        key = jnp.minimum(row_before[j], keys[j] + 3.0)
        result.append(jnp.minimum(key, row_before[j + 3] + 6.0))
    return result, [value[j] for j in range(EDGE, EDGE + step)]


def tally(best, value, out, p, j, add, total):
    sub = lax.broadcasted_iota(jnp.int32, (8, LANES), 0)
    code = best.astype(jnp.int32) & 31
    code = jnp.where(code > 13, code - 1, code)
    bit = jnp.where(best < value, jnp.int32(1) << ((code & 7) * 4), 0)
    kind = code >> 3
    for g in range(-(-out.shape[1] // 8)):
        word = jnp.where(kind == g, bit, 0)
        word = word + pltpu.roll(word, 4, 0)
        word = word + pltpu.roll(word, 2, 0)
        word = word + pltpu.roll(word, 1, 0)
        share = ((word >> (sub * 4)) & 15).astype(jnp.float32) * (1.0 / total)
        n = min(8, out.shape[1] - 8 * g)
        at = (p, slice(8 * g, 8 * g + n), slice(j * LANES, (j + 1) * LANES))
        out[at] = out[at] + share[:n] if add else share[:n]


def inner_kernel(mloc, width, step, total, block, *refs):
    keeps, cames, (tile_out, part, stage) = refs[:mloc], refs[mloc : 2 * mloc], refs[2 * mloc :]
    planes, rows = block.shape[0], block.shape[1]
    first = lax.axis_index("member") % 2 == 1
    for p in range(planes):
        stage[p, 0:rows, :] = block[p].astype(jnp.float32)
    for q in range(keeps[0].shape[0]):
        here = [keep[q].astype(jnp.float32) for keep in keeps]
        there = [came[q].astype(jnp.float32) for came in cames]
        both = [jnp.where(first, a, b) for a, b in zip(here, there)]
        both += [jnp.where(first, b, a) for a, b in zip(here, there)]
        for p in range(planes):
            parts = [value[p * width : (p + 1) * width] for value in both]
            stage[p, (q + 1) * rows : (q + 2) * rows, :] = jnp.concatenate(parts, axis=0)
    for group in range(total // 8):
        layers = []
        for p in range(planes):
            layers.append(keys_of(stage, p, group, width, step, 0))
            if p == 1:
                for j in range(step):
                    part[group, 0, j] = jnp.minimum(layers[0][0][j] + 9.0, layers[1][0][j] + 18.0)
                    part[group, 1, j] = layers[0][1][j]
            if p < 2:
                continue
            for j in range(step):
                best = jnp.minimum(layers[p - 2][0][j], layers[p - 1][0][j] + 9.0)
                best = jnp.minimum(best, layers[p][0][j] + 18.0)
                tally(best, layers[p - 1][1][j], tile_out, p - 2, j, group > 0, total)
        for j in range(step):
            part[group, 2, j] = jnp.minimum(layers[-2][0][j], layers[-1][0][j] + 9.0)
            part[group, 3, j] = layers[-1][1][j]


def half_kernel(wide, step, total, own, *refs):
    *halos, part, source, out, stage, tile_out, sem = refs
    planes = out.shape[0]
    core, last, toward = place()
    later = len(halos) == 2
    end = jnp.where(last, toward, 1 - toward) if later else jnp.where(last, 1 - toward, toward)
    start = core * step
    bias = end.astype(jnp.float32) * 18.0
    copies = []
    if later:
        got, other = halos
        stage[...] = other[...].astype(jnp.float32)
        for rows, owner in ((slice(0, own), 0), (slice(own, got.shape[0]), 1)):

            @pl.when(jnp.logical_and(last, core == owner))
            def _():
                stage[rows, :] = got[rows, :].astype(jnp.float32)
    else:
        copies.append(pltpu.make_async_copy(source, out.at[pl.ds(1, planes - 2)], sem.at[0]))
        copies[0].start()
        stage[...] = halos[0][...].astype(jnp.float32)

        @pl.when(last)
        def _():
            stage[...] = jnp.full(stage.shape, PAD, jnp.float32)

    for group in range(total // 8):
        keys, _ = keys_of(stage, None, group, wide, step, start)
        for j in range(step):
            best = jnp.minimum(part[group, 2 * end, j], keys[j] + bias)
            tally(best, part[group, 2 * end + 1, j], tile_out, 0, j, group > 0, total)
    copies.append(pltpu.make_async_copy(tile_out.at[0], out.at[end * (planes - 1)], sem.at[1]))
    copies[-1].start()
    for copy in copies:
        copy.wait()


def local(members, tiles, fields):
    mloc, planes, cols = fields.shape
    step = cols // members // LANES
    width, wide = step + 2 * EDGE, 2 * step + 2 * EDGE
    spread = cols // LANES
    assert LEAD >= EDGE * mloc
    total = members * mloc
    half = members // 2
    bf16, f32 = jnp.bfloat16, jnp.float32

    def swap(value):
        return permute(value, members, tiles, lambda m, t: (m ^ 1, t))

    view = fields.reshape(mloc, planes, spread, LANES).transpose(1, 2, 0, 3)
    view = view.reshape(planes, spread * mloc, LANES)
    padded = (planes, spread * mloc + 2 * LEAD, LANES)
    early = pl.pallas_call(
        mark_kernel,
        out_shape=jax.ShapeDtypeStruct((8, LANES), f32),
        out_specs=VMEM,
        compiler_params=PARAMS,
        cost_estimate=pl.CostEstimate(flops=1 << 36, bytes_accessed=1 << 24, transcendentals=0),
        name="mark",
    )()
    ours, *sends = pl.pallas_call(
        functools.partial(start_kernel, mloc, wide, step),
        out_shape=[jax.ShapeDtypeStruct(padded, f32)]
        + [jax.ShapeDtypeStruct((planes, mloc * wide, LANES), bf16)] * (half - 1),
        in_specs=[VMEM, VMEM],
        out_specs=[VMEM] * half,
        compiler_params=PARAMS,
        name="load",
    )(view, early)
    theirs = swap(view)
    rim, *edges = pl.pallas_call(
        functools.partial(edges_kernel, mloc, wide, step),
        out_shape=[jax.ShapeDtypeStruct((LEAD, LANES), f32)]
        + [jax.ShapeDtypeStruct((2 * mloc * wide, LANES), bf16)] * half,
        in_specs=[VMEM] * 2,
        out_specs=[VMEM] * (half + 1),
        scratch_shapes=[pltpu.VMEM((2, 1) + padded[1:], f32)],
        compiler_params=PARAMS,
        name="edges",
    )(theirs, ours)
    raws = [permute(sends[q - 1], members, tiles, lambda m, t: (m ^ (2 * q + 1), t)) for q in range(1, half)]
    *raws, rim = lax.optimization_barrier((*raws, rim))
    block = pl.pallas_call(
        functools.partial(block_kernel, mloc, width, step),
        out_shape=jax.ShapeDtypeStruct((planes, 2 * mloc * width, LANES), bf16),
        in_specs=[VMEM] * 3,
        out_specs=VMEM,
        scratch_shapes=[pltpu.VMEM((2,) + padded, f32)],
        compiler_params=PARAMS,
        name="block",
    )(theirs, ours, rim)
    kept = jax.ShapeDtypeStruct((half - 1, planes * width, LANES), bf16)
    crossed = pl.pallas_call(
        functools.partial(cross_kernel, mloc, width, wide, step),
        out_shape=[kept] * (2 * mloc),
        in_specs=[VMEM] * (half - 1),
        out_specs=[VMEM] * (2 * mloc),
        scratch_shapes=[pltpu.VMEM((planes, mloc * wide, LANES), f32)],
        compiler_params=PARAMS,
        name="cross",
    )(*raws)
    keeps, cames = crossed[:mloc], [swap(give) for give in crossed[mloc:]]
    got = [None] * half
    for q in list(range(1, half)) + [0]:
        got[q] = permute(edges[q], members, tiles, functools.partial(beside, q, members, tiles))
    out_shape = jax.ShapeDtypeStruct((planes, 26, step * LANES), f32)
    part_shape = jax.ShapeDtypeStruct((total // 8, 4, step, 8, LANES), f32)
    inner, part = pl.pallas_call(
        functools.partial(inner_kernel, mloc, width, step, total),
        out_shape=[jax.ShapeDtypeStruct((planes - 2, 26, step * LANES), f32), part_shape],
        in_specs=[VMEM] * (1 + 2 * mloc),
        out_specs=[VMEM, VMEM],
        scratch_shapes=[pltpu.VMEM((planes, total * width, LANES), f32)],
        compiler_params=PARAMS,
        name="inner",
    )(block, *keeps, *cames)
    got = pl.pallas_call(
        join_kernel,
        out_shape=jax.ShapeDtypeStruct((total * wide, LANES), bf16),
        in_specs=[VMEM] * half,
        out_specs=VMEM,
        compiler_params=PARAMS,
        name="join",
    )(*got[::-1])
    other = swap(got)
    out = inner
    for halos in ((got,), (got, other)):
        later = len(halos) == 2
        out = pl.pallas_call(
            functools.partial(half_kernel, wide, step, total, 2 * mloc * wide),
            out_shape=out_shape,
            in_specs=[VMEM] * (len(halos) + 1) + [ANY if later else VMEM],
            out_specs=ANY,
            scratch_shapes=[
                pltpu.VMEM((total * wide, LANES), f32),
                pltpu.VMEM((1, 26, step * LANES), f32),
                pltpu.SemaphoreType.DMA((2,)),
            ],
            input_output_aliases={3: 0} if later else {},
            compiler_params=PARAMS,
            name="outer",
        )(*halos, part, out)
    return out.transpose(1, 0, 2)


def solution(mesh):
    sizes = dict(mesh.shape)
    in_specs = (P("member", "tile", None),)
    out_specs = P(None, "tile", "member")
    body = functools.partial(local, sizes["member"], sizes["tile"])
    return jax.shard_map(body, mesh=mesh, in_specs=in_specs, out_specs=out_specs, check_vma=False)
```
